32 devices in a mesh: seq: 4 (over z), phase: 4 (over y, x), dp: 2 (over core).
Axes of the slice: x: 2, y: 2, z: 4, core: 2. Of those that a mesh axis runs over, the one named last changes fastest.
Arguments:
- byte_embed: bfloat16 [4096, 1536], P(('dp', 'seq')), parts along dimension 0, may hold values from -6 to 6
- in_gain: float32 [1536], replicated, may hold values from 0.25 to 1.75
- w_qkv: bfloat16 [1536, 3, 1536], P('seq', None, 'phase')
- w_up: bfloat16 [1536, 3072], P('phase')
- out_gain: float32 [3072], P('phase'), may hold values from 0.25 to 1.75
- bounds: int32 [1024], P(('dp', 'seq')), parts along dimension 0, may hold values from 0 to 2047, as said below
- owner: int32 [1024, 1], P(('dp', 'seq')), parts along dimension 0, may hold values from 0 to 3; in each aligned block of 128 rows (0 to 127, 128 to 255, ...) at most 64 rows name the same one
Outputs:
- byte_states: bfloat16 [4096, 1536], P(('dp', 'seq'), 'phase'), parts along dimension 0
- stretch_states: bfloat16 [2048, 3072], P(('dp', 'seq'), 'phase'), parts along dimension 0
The draws below stay inside these ranges and needn't reach their ends.
There are 2 independent parts, one for each index of `dp`. The reference program is written for one: setup_inputs(seed, part) draws one part's arguments, and reference() takes and returns one part's arrays. A program takes and returns all parts, laid end to end along the dimension named above; an argument that names none is the same for every part. Nothing has to cross between parts.
Inputs may be any that keep to these rules, and one draw needn't show every extreme that they name: `bounds`: strictly rising; the 128 entries of block b lie in bytes b * 512 to (b + 1) * 512 - 1, and the first and last byte of each block are among them. Among the 128 stretch rows of one block no owner is named more than 64 times.
All inputs are finite; a program needn't handle non-finite values.
Results may differ from the reference program's by a relative error of at most 0.013.
Values may be sent and summed in bfloat16 or wider, within the bound.
A program may use at most 128 MiB of HBM per device.

```python
import math
import jax
import jax.numpy as jnp
import numpy as np
from jax import lax

D = 1536
DC = 3072
HD = 128
WINDOW = 1024
TOK_DEV = 512
HEADS = 12
OWNERS = 4
BYTES = 2048
CROWS = 128
SLOT = 64
N_PHASE = 4


def draw_w_qkv(key, part):
    base = jax.random.normal(key, (D, 3, D), jnp.float32) * D ** (-0.5)
    return base.astype(jnp.bfloat16)


def draw_w_up(key, part):
    base = jax.random.normal(jax.random.fold_in(key, 11), (D, DC), jnp.float32) * D ** (-0.5)
    rough = jax.random.uniform(jax.random.fold_in(key, 12), (DC,), jnp.float32, 0.7, 1.3)
    where = jnp.arange(DC, dtype=jnp.float32) / DC
    ramp = jnp.exp(where * 1.3863)
    return (base * (ramp * rough)[None, :]).astype(jnp.bfloat16)


def draw_bounds(key, part):

    def one_block(block):
        sub = jax.random.fold_in(key, block)
        inner = jax.random.permutation(sub, TOK_DEV - 2)[:CROWS - 2].astype(jnp.int32) + 1
        ends = jnp.array([0, TOK_DEV - 1], jnp.int32)
        return jnp.sort(jnp.concatenate([ends, inner])) + block * TOK_DEV
    return jax.vmap(one_block)(jnp.arange(OWNERS, dtype=jnp.int32)).reshape(-1)


def shard_levels(own_key, shape, cuts, least, largest):
    level = 1.0
    for axis_at, shards_of in cuts:
        steps = jax.random.uniform(jax.random.fold_in(jax.random.fold_in(own_key, 6), axis_at), (shards_of,), jnp.float32, least / len(cuts), largest / len(cuts))
        level = level * jnp.repeat(jnp.exp(steps), shape[axis_at] // shards_of).reshape((-1,) + (1,) * (len(shape) - 1 - axis_at))
    return level


def shared_out(rng, own, number, rows, number_of, top, bound, lean):
    sequence = jax.random.permutation(rng, number_of)
    crowded, usual = portions_of(number_of, rows * top, bound, lean, True), portions_of(number_of, rows * top, bound, lean, False)
    places = jnp.arange(number_of)

    def named(lengths, rotation):
        used = int((lengths > 0).sum())
        fixed = max(1, used // 4)
        passed = fixed + (places - fixed + rotation * (used - fixed)) % max(1, number_of - fixed)
        return jnp.zeros((number_of,), jnp.int32).at[sequence[jnp.where(places < fixed, places, passed)]].set(jnp.asarray(lengths, jnp.int32))

    lengths = jnp.where(number % 4 == 0, named(crowded, number // 4), named(usual, number - number // 4 - 1))
    mixed = jax.random.permutation(jax.random.fold_in(own, 3), number_of)
    donor, taker = mixed[0:number_of // 2 * 2:2], mixed[1:number_of // 2 * 2:2]
    room = jnp.minimum(lengths[donor] - 1, bound - lengths[taker]) // 2
    room = jnp.where((donor == sequence[0]) | (taker == sequence[0]) | (lengths[taker] == 0), 0, jnp.maximum(room, 0))
    passed = jax.random.randint(jax.random.fold_in(own, 4), (number_of // 2,), 0, 1 << 20) % (room + 1)
    lengths = lengths.at[donor].add(-passed).at[taker].add(passed)
    items = jnp.searchsorted(jnp.cumsum(lengths), jnp.arange(rows * top), side="right").astype(jnp.int32)
    grid = items.reshape(top, rows).T
    grid = grid[jax.random.permutation(jax.random.fold_in(own, 1), rows)]
    rotation = jax.random.randint(jax.random.fold_in(own, 2), (rows, 1), 0, top)
    return jnp.take_along_axis(grid, (jnp.arange(top)[None, :] + rotation) % top, axis=1)


def portions_of(amount, total, bound, lean, full):
    weights = [(1 << 20) // math.isqrt(grade ** lean) + 1 for grade in range(1, amount + 1)]
    largest = bound if full else min(bound, max(-(-total // amount), total * weights[0] // sum(weights)))
    least = 1 if total - largest >= amount - 1 else 0
    counts, spare = [largest] + [least] * (amount - 1), total - largest - least * (amount - 1)
    while spare > 0:
        movable = [i for i in range(1, amount) if counts[i] < largest] or [i for i in range(1, amount) if counts[i] < bound]
        mass, left = sum([weights[i] for i in movable]), spare
        for i in movable:
            more = min(bound - counts[i], max(1, left * weights[i] // mass), spare)
            counts[i] = counts[i] + more
            spare = spare - more
    return np.array(counts)


def scatter_about(own_key, extent, width, limit, split=(), kind=jnp.bfloat16):
    loudness = shard_levels(own_key, extent, split, -0.22, 0.18) if split else 1.0
    drawn = jax.random.normal(own_key, extent, jnp.float32) * width * loudness
    return jnp.minimum(jnp.maximum(drawn, -limit), limit).astype(kind)


def setup_inputs(seed: int = 0, part: int = 0) -> dict:
    splits = jax.random.split(jax.random.key(seed), 8)
    part_keys = jax.random.split(jax.random.fold_in(splits[7], part), 8)
    byte_embed = scatter_about(part_keys[0], (BYTES, D), 1.0, 6.0, ((0, 4),))
    in_gain = jnp.clip(1.0 + 0.15 * jax.random.normal(splits[1], (D,), jnp.float32), 0.25, 1.75)
    w_qkv = draw_w_qkv(jax.random.fold_in(splits[7], 71), part)
    w_up = draw_w_up(jax.random.fold_in(splits[7], 71), part)
    out_gain = jnp.clip(1.0 + 0.15 * jax.random.normal(splits[4], (DC,), jnp.float32), 0.25, 1.75)
    bounds = draw_bounds(jax.random.fold_in(jax.random.fold_in(splits[7], part), 71), part)
    owner_keys = jax.random.split(jax.random.fold_in(part_keys[6], 1), (OWNERS * CROWS) // CROWS)
    owner_turns = jax.random.permutation(jax.random.fold_in(part_keys[6], 3), (OWNERS * CROWS) // CROWS)
    owner = jax.vmap(lambda own, number: shared_out(jax.random.fold_in(part_keys[6], 2), own, number, CROWS, OWNERS, 1, SLOT, 2))(owner_keys, owner_turns).reshape((OWNERS * CROWS, 1))
    return dict(byte_embed=byte_embed, in_gain=in_gain, w_qkv=w_qkv, w_up=w_up, out_gain=out_gain, bounds=bounds, owner=owner)


def reference(byte_embed, in_gain, w_qkv, w_up, out_gain, bounds, owner):
    x32 = byte_embed.astype(jnp.float32)
    normed = (x32 * lax.rsqrt(lax.optimization_barrier(jnp.mean(x32 * x32, axis=1, keepdims=True)) + 1e-05) * in_gain).astype(jnp.bfloat16)
    qkv = jnp.dot(normed, w_qkv.reshape(D, 3 * D), preferred_element_type=jnp.float32).astype(jnp.bfloat16)
    qkv = qkv.reshape(BYTES, 3, HEADS, HD)
    query = qkv[:, 0]
    keys = qkv[:, 1]
    values = qkv[:, 2]
    padding = jnp.zeros((WINDOW, HEADS, HD), jnp.bfloat16)
    keys_pad = jnp.concatenate([padding, keys], axis=0)
    values_pad = jnp.concatenate([padding, values], axis=0)
    span = WINDOW + TOK_DEV

    def block(index):
        start = (index * TOK_DEV).astype(jnp.int32)
        q_blk = lax.dynamic_slice_in_dim(query, start, TOK_DEV, 0).astype(jnp.float32)
        k_blk = lax.dynamic_slice_in_dim(keys_pad, start, span, 0).astype(jnp.float32)
        v_blk = lax.dynamic_slice_in_dim(values_pad, start, span, 0).astype(jnp.float32)
        scores = jnp.einsum('ihd,jhd->hij', q_blk, k_blk) * HD ** (-0.5)
        q_pos = start + jnp.arange(TOK_DEV, dtype=jnp.int32)
        k_pos = start - WINDOW + jnp.arange(span, dtype=jnp.int32)
        keep = (k_pos[None, :] <= q_pos[:, None]) & (k_pos[None, :] > q_pos[:, None] - WINDOW) & (k_pos[None, :] >= 0)
        scores = jnp.where(keep[None], scores, -jnp.inf)
        top = lax.optimization_barrier(jnp.max(scores, axis=2, keepdims=True))
        expo = jnp.exp(scores - top)
        probs = (expo / lax.optimization_barrier(jnp.sum(expo, axis=2, keepdims=True))).astype(jnp.bfloat16)
        return jnp.einsum('hij,jhd->ihd', probs.astype(jnp.float32), v_blk).astype(jnp.bfloat16)
    attended = lax.map(block, jnp.arange(OWNERS, dtype=jnp.int32)).reshape(BYTES, D)
    byte_states = (x32 + attended.astype(jnp.float32)).astype(jnp.bfloat16)
    stretch_rows = byte_states[bounds]
    group = D // N_PHASE
    projected = jnp.zeros((OWNERS * CROWS, DC), jnp.float32)
    for part in range(N_PHASE):
        piece = jnp.dot(stretch_rows[:, part * group:(part + 1) * group], w_up[part * group:(part + 1) * group], preferred_element_type=jnp.float32)
        projected = projected + piece.astype(jnp.bfloat16).astype(jnp.float32)
    main_in = (projected * lax.rsqrt(lax.optimization_barrier(jnp.mean(projected * projected, axis=1, keepdims=True)) + 1e-05) * out_gain).astype(jnp.bfloat16)
    owners = owner[:, 0].reshape(OWNERS, CROWS)
    place = jnp.arange(CROWS, dtype=jnp.int32)
    earlier = (owners[:, :, None] == owners[:, None, :]) & (place[None, None, :] < place[None, :, None])
    rank = lax.optimization_barrier(jnp.sum(earlier.astype(jnp.int32), axis=2))
    source = jnp.arange(OWNERS, dtype=jnp.int32)[:, None]
    target = (owners * (OWNERS * SLOT) + source * SLOT + rank).reshape(-1)
    stretch_states = jnp.zeros((OWNERS * OWNERS * SLOT, DC), jnp.bfloat16).at[target].set(main_in)
    return (byte_states, stretch_states)
```

```python
import functools
import math
import jax
import jax.numpy as jnp
from jax import lax
from jax.experimental import pallas as pl
from jax.experimental.pallas import tpu as pltpu
from jax.sharding import PartitionSpec as P

DC = 3072
HD = 128
WINDOW = 1024
MESH = pl.DeviceIdType.MESH
NEG = -0.7 * 3.4e38


def fused_kernel(
    dims,
    x_ref,
    gain_ref,
    w_ref,
    up_ref,
    og_ref,
    bounds_ref,
    ocol_ref,
    orow_ref,
    bs_ref,
    ss_ref,
    wbuf,
    upbuf,
    normed,
    acc,
    qbuf,
    kbuf,
    vbuf,
    obuf,
    mbuf,
    lbuf,
    rowbuf,
    sqbuf,
    outbuf,
    loc_sem,
    w_send,
    w_recv,
    p_send,
    p_recv,
    up_send,
    up_recv,
    kv_send,
    kv_recv,
    row_send,
    row_recv,
    sq_send,
    sq_recv,
    a_send,
    a_recv,
):
    n_seq, n_phase, reach, slot = dims
    tok, d = x_ref.shape
    rows = w_ref.shape[0]
    half = rows // 2
    width = w_ref.shape[1] // 3
    heads = width // HD
    crows = bounds_ref.shape[0]
    cols = og_ref.shape[1]
    z = lax.axis_index("seq")
    p = lax.axis_index("phase")
    c = lax.axis_index("dp")

    peers = (
        [{"seq": lax.rem(z + k, n_seq)} for k in range(1, n_seq)]
        + [{"phase": lax.rem(p + k, n_phase)} for k in range(1, n_phase)]
        + [{"dp": 1 - c}]
    )
    barrier = pltpu.get_barrier_semaphore()
    for peer in peers:
        pl.semaphore_signal(barrier, inc=1, device_id=peer, device_id_type=MESH)
    pl.semaphore_wait(barrier, len(peers))

    pending = []

    def send(src, dst, ssem, rsem, peer, cond=None):
        copy = pltpu.make_async_remote_copy(
            src_ref=src, dst_ref=dst, send_sem=ssem, recv_sem=rsem, device_id=peer, device_id_type=MESH
        )
        if cond is None:
            copy.start()
        else:
            pl.when(cond)(copy.start)
        pending.append((cond, copy))
        return copy

    mine_half = pl.ds(pl.multiple_of(c * half, half), half)
    right, left = {"seq": z + 1}, {"seq": z - 1}
    ways = ((right, z < n_seq - 1, -1), (left, z > 0, 1))
    for way, (peer, cond, sign) in enumerate(ways):
        send(
            w_ref.at[mine_half],
            wbuf.at[z, mine_half],
            w_send.at[way, 0],
            w_recv.at[way, 0],
            peer,
            cond,
        )
    own_w = pltpu.make_async_copy(w_ref, wbuf.at[z], loc_sem.at[0])
    own_w.start()
    up_copies = []
    for k in range(1, n_phase):
        other = lax.rem(p + k, n_phase)
        part = pl.ds(pl.multiple_of(other * cols, 128), cols)
        up_copies.append(
            send(up_ref.at[:, part], upbuf.at[p], up_send.at[k - 1], up_recv.at[k - 1], {"phase": other})
        )
    own_up = pltpu.make_async_copy(
        up_ref.at[:, pl.ds(pl.multiple_of(p * cols, 128), cols)], upbuf.at[p], loc_sem.at[1]
    )
    own_up.start()

    step_rows = 64

    @pl.loop(0, tok // step_rows)
    def _(i):
        r = pl.ds(pl.multiple_of(i * step_rows, step_rows), step_rows)
        xx = x_ref[r, :].astype(jnp.float32)
        scale = lax.rsqrt(jnp.mean(xx * xx, axis=1, keepdims=True) + 1e-05)
        normed[r, :] = (xx * scale * gain_ref[...]).astype(jnp.bfloat16)

    def accumulate(shard, first):
        k = pl.ds(pl.multiple_of(shard * rows, 128), rows)

        @pl.loop(0, 3)
        def _(j):
            n = pl.ds(pl.multiple_of(j * width, 128), width)
            part = jnp.dot(normed[:, k], wbuf[shard, :, n], preferred_element_type=jnp.float32)
            if first:
                acc[:, n] = part
            else:
                acc[:, n] = acc[:, n] + part

    own_w.wait()
    accumulate(z, True)

    for t in range(1, n_seq):
        arrivals = []
        for way, (peer, cond, sign) in enumerate(ways):
            shard = z + sign * t
            there = (shard >= 0) & (shard < n_seq)
            piece = wbuf.at[jnp.clip(shard, 0, n_seq - 1), mine_half]
            got = pltpu.make_async_remote_copy(
                src_ref=piece,
                dst_ref=piece,
                send_sem=w_send.at[way, t - 1],
                recv_sem=w_recv.at[way, t - 1],
                device_id=peer,
                device_id_type=MESH,
            )
            pl.when(there)(got.wait_recv)
            if t < n_seq - 1:
                send(piece, piece, w_send.at[way, t], w_recv.at[way, t], peer, there & cond)
            twin = send(piece, piece, p_send.at[way, t - 1], p_recv.at[way, t - 1], {"dp": 1 - c}, there)
            arrivals.append((there, shard, twin))
        for there, shard, twin in arrivals:

            @pl.when(there)
            def _():
                twin.wait_recv()
                accumulate(shard, False)

    for h in range(heads):
        kbuf[0, h] = acc[:, width + h * HD : width + (h + 1) * HD].astype(jnp.bfloat16)
    for h in range(heads):
        vbuf[0, h] = acc[:, 2 * width + h * HD : 2 * width + (h + 1) * HD].astype(jnp.bfloat16)
    has_right = z < n_seq - 1
    kv_copies = {}

    def send_kv(dist, cond):
        for which, buf in enumerate((kbuf, vbuf)):
            kv_copies[dist, which] = send(
                buf.at[dist], buf.at[dist + 1], kv_send.at[which, dist], kv_recv.at[which, dist], right, cond
            )

    send_kv(0, has_right)
    for h in range(heads):
        qbuf[h] = acc[:, h * HD : (h + 1) * HD].astype(jnp.bfloat16)

    tq = min(tok, 256)
    scale = HD ** (-0.5) * math.log2(math.e)

    def attend(dist):
        @pl.loop(0, heads * (tok // tq))
        def _(it):
            h = it // (tok // tq)
            q0 = pl.multiple_of((it % (tok // tq)) * tq, tq)
            r = pl.ds(q0, tq)
            s = lax.dot_general(
                qbuf[h, r, :],
                kbuf[dist, h],
                (((1,), (1,)), ((), ())),
                preferred_element_type=jnp.float32,
            )
            if dist == 0 or (dist + 1) * tok - 1 >= WINDOW:
                qi = q0 + lax.broadcasted_iota(jnp.int32, s.shape, 0)
                kj = lax.broadcasted_iota(jnp.int32, s.shape, 1) - dist * tok
                s = jnp.where((kj <= qi) & (kj > qi - WINDOW), s, NEG)
            top = jnp.max(s, axis=1, keepdims=True)
            if dist > 0:
                old = mbuf[h, r, :]
                top = jnp.maximum(top, old)
            e = jnp.exp2(s * scale - top * scale)
            total = jnp.sum(e, axis=1, keepdims=True)
            o = jnp.dot(e.astype(jnp.bfloat16), vbuf[dist, h], preferred_element_type=jnp.float32)
            if dist > 0:
                fade = jnp.exp2((old - top) * scale)
                total = total + fade * lbuf[h, r, :]
                o = o + fade * obuf[h, r, :]
            mbuf[h, r, :] = top
            lbuf[h, r, :] = total
            obuf[h, r, :] = o

    attend(0)
    for dist in range(1, reach + 1):
        there = z >= dist

        @pl.when(there)
        def _():
            for which in range(2):
                kv_copies[dist - 1, which].wait_recv()

        if dist < reach:
            send_kv(dist, there & has_right)

        @pl.when(there)
        def _():
            attend(dist)

    for h in range(heads):
        res = x_ref[:, pl.ds(pl.multiple_of(p * width + h * HD, HD), HD)].astype(jnp.float32)
        att = (obuf[h] / lbuf[h]).astype(jnp.bfloat16).astype(jnp.float32)
        bs_ref[:, h * HD : (h + 1) * HD] = (res + att).astype(jnp.bfloat16)

    local = bounds_ref[...] - z * tok
    pick = (local == lax.broadcasted_iota(jnp.int32, (crows, tok), 1)).astype(jnp.float32).astype(jnp.bfloat16)
    rowbuf[p] = jnp.dot(pick, bs_ref[...], preferred_element_type=jnp.float32).astype(jnp.bfloat16)
    row_copies = []
    for k in range(1, n_phase):
        other = lax.rem(p + k, n_phase)
        row_copies.append(
            send(rowbuf.at[p], rowbuf.at[p], row_send.at[k - 1], row_recv.at[k - 1], {"phase": other})
        )

    same = ocol_ref[...] == orow_ref[...]
    before = lax.broadcasted_iota(jnp.int32, (crows, crows), 0) < lax.broadcasted_iota(
        jnp.int32, (crows, crows), 1
    )
    rank = jnp.sum(jnp.where(same & before, 1, 0), axis=0, keepdims=True)
    target = orow_ref[...] * slot + rank
    place = (target == lax.broadcasted_iota(jnp.int32, (n_seq * slot, crows), 0)).astype(jnp.float32).astype(
        jnp.bfloat16
    )

    own_up.wait()
    for copy in up_copies:
        copy.wait_recv()

    def piece(s):
        got = jnp.dot(rowbuf[s], upbuf[s], preferred_element_type=jnp.float32)
        return got.astype(jnp.bfloat16).astype(jnp.float32)

    projected = piece(p)
    for copy in row_copies:
        copy.wait_recv()
    for k in range(1, n_phase):
        projected = projected + piece(lax.rem(p + k, n_phase))
    sq = jnp.sum(projected * projected, axis=1, keepdims=True)
    sqbuf[p] = jnp.broadcast_to(sq, (crows, crows)).T[0:8, :]
    sq_copies = []
    for k in range(1, n_phase):
        other = lax.rem(p + k, n_phase)
        sq_copies.append(
            send(sqbuf.at[p], sqbuf.at[p], sq_send.at[k - 1], sq_recv.at[k - 1], {"phase": other})
        )
    for copy in sq_copies:
        copy.wait_recv()
    all_sq = sqbuf[0]
    for k in range(1, n_phase):
        all_sq = all_sq + sqbuf[k]
    all_sq = jnp.broadcast_to(all_sq[0:1, :], (crows, crows)).T[:, 0:1]
    norm = lax.rsqrt(all_sq / (n_phase * cols) + 1e-05)
    main_in = (projected * norm * og_ref[...]).astype(jnp.bfloat16)
    routed = jnp.dot(place, main_in, preferred_element_type=jnp.float32).astype(jnp.bfloat16)
    for s in range(n_seq):
        outbuf[s] = routed[s * slot : (s + 1) * slot]
    a_copies = []
    for k in range(1, n_seq):
        other = lax.rem(z + k, n_seq)
        a_copies.append(
            send(outbuf.at[other], ss_ref.at[z], a_send.at[k - 1], a_recv.at[k - 1], {"seq": other})
        )
    ss_ref[z] = outbuf[z]
    for copy in a_copies:
        copy.wait_recv()
    for cond, copy in pending:
        if cond is None:
            copy.wait_send()
        else:
            pl.when(cond)(copy.wait_send)


def fused(n_seq, n_phase, byte_embed, in_gain, w_qkv, w_up, out_gain, bounds, owner):
    tok, d = byte_embed.shape
    rows, _, width = w_qkv.shape
    heads = width // HD
    crows = bounds.shape[0]
    cols = out_gain.shape[0]
    slot = 2 * crows // n_seq
    reach = -(-WINDOW // tok)
    bf, f32 = jnp.bfloat16, jnp.float32
    vmem = pl.BlockSpec(memory_space=pltpu.VMEM)
    hbm = pl.BlockSpec(memory_space=pl.ANY)
    dma = pltpu.SemaphoreType.DMA
    states, stretch = pl.pallas_call(
        functools.partial(fused_kernel, (n_seq, n_phase, reach, slot)),
        out_shape=(
            jax.ShapeDtypeStruct((tok, width), bf),
            jax.ShapeDtypeStruct((n_seq, slot, cols), bf),
        ),
        in_specs=[vmem, vmem, hbm, hbm, vmem, vmem, vmem, vmem],
        out_specs=(vmem, vmem),
        scratch_shapes=[
            pltpu.VMEM((n_seq, rows, 3 * width), bf),
            pltpu.VMEM((n_phase, rows, cols), bf),
            pltpu.VMEM((tok, d), bf),
            pltpu.VMEM((tok, 3 * width), f32),
            pltpu.VMEM((heads, tok, HD), bf),
            pltpu.VMEM((reach + 1, heads, tok, HD), bf),
            pltpu.VMEM((reach + 1, heads, tok, HD), bf),
            pltpu.VMEM((heads, tok, HD), f32),
            pltpu.VMEM((heads, tok, 1), f32),
            pltpu.VMEM((heads, tok, 1), f32),
            pltpu.VMEM((n_phase, crows, width), bf),
            pltpu.VMEM((n_phase, 8, crows), f32),
            pltpu.VMEM((n_seq, slot, cols), bf),
            dma((2,)),
            dma((2, n_seq - 1)),
            dma((2, n_seq - 1)),
            dma((2, n_seq - 1)),
            dma((2, n_seq - 1)),
            dma((n_phase - 1,)),
            dma((n_phase - 1,)),
            dma((2, reach)),
            dma((2, reach)),
            dma((n_phase - 1,)),
            dma((n_phase - 1,)),
            dma((n_phase - 1,)),
            dma((n_phase - 1,)),
            dma((n_seq - 1,)),
            dma((n_seq - 1,)),
        ],
        compiler_params=pltpu.CompilerParams(
            collective_id=0, has_side_effects=True, vmem_limit_bytes=48 * 1024 * 1024
        ),
    )(
        byte_embed,
        in_gain.reshape(1, d),
        w_qkv.reshape(rows, 3 * width),
        w_up,
        out_gain.reshape(1, cols),
        bounds.reshape(crows, 1),
        owner,
        owner.reshape(1, crows),
    )
    return states, stretch.reshape(n_seq * slot, cols)


def passed_along(value, axis, by):
    devices = lax.axis_size(axis)
    pairs = [(i, i + by) for i in range(devices) if 0 <= i + by < devices]
    return lax.ppermute(value, axis, pairs)


def project_rows(rows, w_up, out_gain):
    groups = lax.axis_size("phase")
    full_rows = lax.all_gather(rows, "phase", axis=1, tiled=True)
    w_cols = lax.all_to_all(w_up, "phase", split_axis=1, concat_axis=0, tiled=True)
    count = full_rows.shape[0]
    width = rows.shape[1]
    columns = w_cols.shape[1]
    pieces = jnp.einsum(
        "nsg,sgc->snc",
        full_rows.reshape(count, groups, width),
        w_cols.reshape(groups, width, columns),
        preferred_element_type=jnp.float32,
    )
    projected = jnp.sum(pieces.astype(jnp.bfloat16).astype(jnp.float32), axis=0)
    squares = lax.psum(jnp.sum(projected * projected, axis=1), "phase")
    scale = lax.rsqrt(squares / DC + 1e-05)
    return (projected * scale[:, None] * out_gain).astype(jnp.bfloat16)


def on_device(byte_embed, in_gain, w_qkv, w_up, out_gain, bounds, owner):
    tok = byte_embed.shape[0]
    n_seq = lax.axis_size("seq")
    mine = lax.axis_index("seq")
    section = lax.axis_index("phase")
    width_dev = w_qkv.shape[2]
    heads_dev = width_dev // HD
    x32 = byte_embed.astype(jnp.float32)
    normed = (x32 * lax.rsqrt(jnp.mean(x32 * x32, axis=1, keepdims=True) + 1e-05) * in_gain).astype(
        jnp.bfloat16
    )
    piece = lax.all_gather(w_qkv, "seq", axis=0, tiled=True)
    qkv = jnp.dot(
        normed, piece.reshape(piece.shape[0], 3 * width_dev), preferred_element_type=jnp.float32
    ).astype(jnp.bfloat16)
    qkv = qkv.reshape(tok, 3, heads_dev, HD)
    query = qkv[:, 0]
    keys = qkv[:, 1]
    values = qkv[:, 2]
    reach = -(-WINDOW // tok)
    key_list = [keys]
    value_list = [values]
    for distance in range(1, reach + 1):
        earlier_keys, earlier_values = passed_along((keys, values), "seq", distance)
        key_list = [earlier_keys] + key_list
        value_list = [earlier_values] + value_list
    key_all = jnp.concatenate(key_list, axis=0)
    value_all = jnp.concatenate(value_list, axis=0)
    scores = jnp.einsum(
        "ihd,jhd->hij", query, key_all, preferred_element_type=jnp.float32
    ) * HD ** (-0.5)
    q_pos = mine * tok + jnp.arange(tok, dtype=jnp.int32)
    k_pos = mine * tok - reach * tok + jnp.arange((reach + 1) * tok, dtype=jnp.int32)
    keep = (
        (k_pos[None, :] <= q_pos[:, None])
        & (k_pos[None, :] > q_pos[:, None] - WINDOW)
        & (k_pos[None, :] >= 0)
    )
    scores = jnp.where(keep[None], scores, -jnp.inf)
    top = jnp.max(scores, axis=2, keepdims=True)
    expo = jnp.exp(scores - top)
    probs = (expo / jnp.sum(expo, axis=2, keepdims=True)).astype(jnp.bfloat16)
    attended = jnp.einsum(
        "hij,jhd->ihd", probs, value_all, preferred_element_type=jnp.float32
    ).astype(jnp.bfloat16)
    attended = attended.reshape(tok, width_dev)
    residual = lax.dynamic_slice_in_dim(x32, section * width_dev, width_dev, 1)
    byte_states = (residual + attended.astype(jnp.float32)).astype(jnp.bfloat16)
    local = bounds - mine * tok
    stretch_rows = jnp.take(byte_states, local, axis=0)
    owners = owner[:, 0]
    crows = owners.shape[0]
    slot_count = 2 * crows // n_seq
    place = jnp.arange(crows, dtype=jnp.int32)
    earlier = (owners[:, None] == owners[None, :]) & (place[None, :] < place[:, None])
    rank = jnp.sum(earlier.astype(jnp.int32), axis=1)
    target = owners * slot_count + rank
    placing = (target[None, :] == jnp.arange(n_seq * slot_count, dtype=jnp.int32)[:, None]).astype(
        jnp.bfloat16
    )
    outgoing = jnp.dot(placing, stretch_rows, preferred_element_type=jnp.float32).astype(
        jnp.bfloat16
    )
    outgoing = outgoing.reshape(n_seq, slot_count, width_dev)
    arrived = lax.all_to_all(outgoing, "seq", split_axis=0, concat_axis=0, tiled=True).reshape(
        n_seq * slot_count, width_dev
    )
    stretch_states = project_rows(arrived, w_up, out_gain)
    return (byte_states, stretch_states)


def solution(mesh):
    n_seq, n_phase, n_dp = (mesh.shape[axis] for axis in ("seq", "phase", "dp"))

    def body(byte_embed, in_gain, w_qkv, *rest):
        tok, (rows, _, width) = byte_embed.shape[0], w_qkv.shape
        slot = 2 * rest[2].shape[0] // n_seq
        tiled = rows % 128 == 0 and width % HD == 0 and tok % 256 == 0 and slot % 16 == 0
        if tiled and n_dp == 2 and w_qkv.shape[0] == rest[0].shape[0]:
            return fused(n_seq, n_phase, byte_embed, in_gain, w_qkv, *rest)
        return on_device(byte_embed, in_gain, w_qkv, *rest)

    return jax.shard_map(
        body,
        mesh=mesh,
        in_specs=(
            P(("dp", "seq"), None),
            P(),
            P("seq", None, "phase"),
            P("phase", None),
            P("phase"),
            P(("dp", "seq")),
            P(("dp", "seq"), None),
        ),
        out_specs=(P(("dp", "seq"), "phase"), P(("dp", "seq"), "phase")),
        check_vma=False,
    )
```

```python
import functools
import math
import jax
import jax.numpy as jnp
from jax import lax
from jax.experimental import pallas as pl
from jax.experimental.pallas import tpu as pltpu
from jax.sharding import PartitionSpec as P

DC = 3072
HD = 128
WINDOW = 1024
MESH = pl.DeviceIdType.MESH
NEG = -0.7 * 3.4e38


def fused_kernel(
    dims,
    x_ref,
    gain_ref,
    w_ref,
    up_ref,
    og_ref,
    bounds_ref,
    owner_ref,
    bs_ref,
    ss_ref,
    xbuf,
    normed,
    halo,
    nhalo,
    wbuf,
    upbuf,
    kbuf,
    vbuf,
    obuf,
    mbuf,
    lbuf,
    rowbuf,
    sqbuf,
    outbuf,
    loc_sem,
    w_send,
    w_recv,
    p_send,
    p_recv,
    up_send,
    up_recv,
    upp_send,
    upp_recv,
    h_send,
    h_recv,
    g_send,
    g_recv,
    row_send,
    row_recv,
    sq_send,
    sq_recv,
    a_send,
    a_recv,
):
    n_seq, n_phase, reach, slot = dims
    tok, d = xbuf.shape
    rows, width = w_ref.shape[1:]
    half = rows // 2
    heads = width // HD
    crows = bounds_ref.shape[1]
    cols = og_ref.shape[1]
    z = lax.axis_index("seq")
    p = lax.axis_index("phase")
    c = lax.axis_index("dp")

    own_x = pltpu.make_async_copy(x_ref, xbuf, loc_sem.at[0])
    own_x.start()
    own_up = pltpu.make_async_copy(
        up_ref.at[:, pl.ds(pl.multiple_of(p * cols, 128), cols)], upbuf.at[p], loc_sem.at[1]
    )
    own_up.start()
    own_w = []
    for h in range(heads):
        own_w.append(
            pltpu.make_async_copy(
                w_ref.at[:, :, pl.ds(h * HD, HD)],
                wbuf.at[h, :, pl.ds(pl.multiple_of(z * rows, rows), rows), :],
                loc_sem.at[2 + h],
            )
        )
        own_w[h].start()

    twin_core = {"dp": 1 - c}
    peers = (
        [{"seq": lax.rem(z + k, n_seq)} for k in range(1, n_seq)]
        + [{"phase": lax.rem(p + k, n_phase)} for k in range(1, n_phase)]
        + [twin_core]
    )
    barrier = pltpu.get_barrier_semaphore()
    for peer in peers:
        pl.semaphore_signal(barrier, inc=1, device_id=peer, device_id_type=MESH)
    pl.semaphore_wait(barrier, len(peers))

    pending = []

    def when(cond, action):
        if cond is None:
            action()
        else:
            pl.when(cond)(action)

    def send(src, dst, ssem, rsem, peer, cond=None):
        copy = pltpu.make_async_remote_copy(
            src_ref=src, dst_ref=dst, send_sem=ssem, recv_sem=rsem, device_id=peer, device_id_type=MESH
        )
        when(cond, copy.start)
        pending.append((cond, copy))
        return copy

    right, left = {"seq": z + 1}, {"seq": z - 1}
    has_right, has_left = z < n_seq - 1, z > 0
    ways = ((right, has_right, -1), (left, has_left, 1))

    def chunk(h, shard):
        at = pl.multiple_of(shard * rows + c * half, half)
        return wbuf.at[h, :, pl.ds(at, half), :]

    def issue_own(h):
        src = w_ref.at[:, pl.ds(pl.multiple_of(c * half, half), half), pl.ds(h * HD, HD)]
        for way, (peer, cond, sign) in enumerate(ways):
            send(src, chunk(h, z), w_send.at[way, h, 0], w_recv.at[way, h, 0], peer, cond)

    twins = {}

    def relay(h, t):
        for way, (peer, cond, sign) in enumerate(ways):
            shard = z + sign * t
            there = (shard >= 0) & (shard < n_seq)
            piece = chunk(h, jnp.clip(shard, 0, n_seq - 1))
            got = pltpu.make_async_remote_copy(
                src_ref=piece,
                dst_ref=piece,
                send_sem=w_send.at[way, h, t - 1],
                recv_sem=w_recv.at[way, h, t - 1],
                device_id=peer,
                device_id_type=MESH,
            )
            pl.when(there)(got.wait_recv)
            if t < n_seq - 1:
                send(piece, piece, w_send.at[way, h, t], w_recv.at[way, h, t], peer, there & cond)
            twins[h, t, way] = (
                there,
                send(piece, piece, p_send.at[way, h, t - 1], p_recv.at[way, h, t - 1], twin_core, there),
            )

    def finish(h):
        own_w[h].wait()
        for t in range(1, n_seq):
            for way in range(2):
                there, twin = twins[h, t, way]
                pl.when(there)(twin.wait_recv)

    across = {1: {"phase": p + 1 - 2 * lax.rem(p, 2)}, 2: {"phase": lax.rem(p + 2, n_phase)}}
    spots = {k: v["phase"] for k, v in across.items()}
    mine = {}

    def halo_start(dist, cond):
        src = x_ref.at[:, pl.ds(pl.multiple_of(p * width, 128), width)] if dist == 1 else halo.at[dist - 2, p]
        mine[dist] = send(src, halo.at[dist - 1, p], h_send.at[dist - 1], h_recv.at[dist - 1], right, cond)

    gathers = {}

    def halo_spread(dist):
        there = z >= dist
        pl.when(there)(mine[dist].wait_recv)
        if dist < reach:
            halo_start(dist + 1, there & has_right)
        for k in (1, 2):
            piece = halo.at[dist - 1, p]
            gathers[dist, k] = send(
                piece, piece, g_send.at[dist - 1, k - 1], g_recv.at[dist - 1, k - 1], across[k], there
            )

    def halo_pass(dist):
        there = z >= dist
        for k in (1, 2):
            pl.when(there)(gathers[dist, k].wait_recv)
            part = pl.ds((k - 1) * (tok // 2), tok // 2)
            piece = halo.at[dist - 1, spots[k], part]
            gathers[dist, 2 + k] = send(
                piece, piece, g_send.at[dist - 1, k + 1], g_recv.at[dist - 1, k + 1], across[3 - k], there
            )

    step_rows = 64

    def halo_norm(dist):
        @pl.when(z >= dist)
        def _():
            for k in (1, 2):
                gathers[dist, 2 + k].wait_recv()

            @pl.loop(0, tok // step_rows)
            def _(i):
                r = pl.ds(pl.multiple_of(i * step_rows, step_rows), step_rows)
                xx = jnp.concatenate([halo[dist - 1, s, r, :] for s in range(n_phase)], axis=1).astype(
                    jnp.float32
                )
                scale = lax.rsqrt(jnp.mean(xx * xx, axis=1, keepdims=True) + 1e-05)
                nhalo[dist - 1, r, :] = (xx * scale * gain_ref[...]).astype(jnp.bfloat16)

    halo_start(1, has_right)
    issue_own(0)
    up_rows = up_ref.shape[0] // 2
    up_half = pl.ds(pl.multiple_of(c * up_rows, up_rows), up_rows)
    up_copies, up_twins = [], []
    for k in range(1, n_phase):
        other = lax.rem(p + k, n_phase)
        part = pl.ds(pl.multiple_of(other * cols, 128), cols)
        up_copies.append(
            send(
                up_ref.at[up_half, part],
                upbuf.at[p, up_half],
                up_send.at[k - 1],
                up_recv.at[k - 1],
                {"phase": other},
            )
        )

    own_x.wait()

    @pl.loop(0, tok // step_rows)
    def _(i):
        r = pl.ds(pl.multiple_of(i * step_rows, step_rows), step_rows)
        xx = xbuf[r, :].astype(jnp.float32)
        scale = lax.rsqrt(jnp.mean(xx * xx, axis=1, keepdims=True) + 1e-05)
        normed[r, :] = (xx * scale * gain_ref[...]).astype(jnp.bfloat16)

    def column(ref):
        wide = jnp.broadcast_to(ref[...].astype(jnp.float32), (crows, crows))
        return wide.T

    local = column(bounds_ref)[:, 0:1] - (z * tok).astype(jnp.float32)
    spot = lax.broadcasted_iota(jnp.int32, (crows, tok), 1).astype(jnp.float32)
    pick = jnp.where(local == spot, 1.0, 0.0).astype(jnp.bfloat16)
    same = column(owner_ref) == owner_ref[...].astype(jnp.float32)
    before = lax.broadcasted_iota(jnp.int32, (crows, crows), 0) < lax.broadcasted_iota(
        jnp.int32, (crows, crows), 1
    )
    rank = jnp.sum(jnp.where(same & before, 1, 0), axis=0, keepdims=True)
    target = owner_ref[...] * slot + rank
    place = jnp.where(
        target == lax.broadcasted_iota(jnp.int32, (n_seq * slot, crows), 0), 1.0, 0.0
    ).astype(jnp.bfloat16)

    tq = min(tok, 256)
    scale = HD ** (-0.5) * math.log2(math.e)

    def attend(dist, query):
        for q0 in range(0, tok, tq):
            r = pl.ds(q0, tq)
            keys = tok if dist else q0 + tq
            s = lax.dot_general(
                query[q0 : q0 + tq],
                kbuf[dist, :keys],
                (((1,), (1,)), ((), ())),
                preferred_element_type=jnp.float32,
            )
            if dist == 0 or (dist + 1) * tok - 1 >= WINDOW:
                qi = q0 + lax.broadcasted_iota(jnp.int32, s.shape, 0)
                kj = lax.broadcasted_iota(jnp.int32, s.shape, 1) - dist * tok
                s = jnp.where((kj <= qi) & (kj > qi - WINDOW), s, NEG)
            top = jnp.max(s, axis=1, keepdims=True)
            if dist > 0:
                old = mbuf[r, :]
                top = jnp.maximum(top, old)
            e = jnp.exp2(s * scale - top * scale)
            total = jnp.sum(e, axis=1, keepdims=True)
            o = jnp.dot(e.astype(jnp.bfloat16), vbuf[dist, :keys], preferred_element_type=jnp.float32)
            if dist > 0:
                fade = jnp.exp2((old - top) * scale)
                total = total + fade * lbuf[r, :]
                o = o + fade * obuf[r, :]
            mbuf[r, :] = top
            lbuf[r, :] = total
            obuf[r, :] = o

    def own_block(h):
        w = jnp.concatenate([wbuf[h, j] for j in range(3)], axis=1)
        got = jnp.dot(normed[...], w, preferred_element_type=jnp.float32).astype(jnp.bfloat16)
        qbuf = got[:, :HD]
        kbuf[0] = got[:, HD : 2 * HD]
        vbuf[0] = got[:, 2 * HD :]
        attend(0, qbuf)
        return qbuf

    def earlier_block(h, dist, query):
        @pl.when(z >= dist)
        def _():
            w = jnp.concatenate([wbuf[h, j] for j in range(1, 3)], axis=1)
            got = jnp.dot(nhalo[dist - 1], w, preferred_element_type=jnp.float32).astype(jnp.bfloat16)
            kbuf[dist] = got[:, :HD]
            vbuf[dist] = got[:, HD:]
            attend(dist, query)

    row_copies = []

    def close(h):
        at = slice(h * HD, (h + 1) * HD)
        res = xbuf[:, pl.ds(pl.multiple_of(p * width + h * HD, HD), HD)].astype(jnp.float32)
        att = (obuf[...] / lbuf[...]).astype(jnp.bfloat16).astype(jnp.float32)
        states = (res + att).astype(jnp.bfloat16)
        bs_ref[:, at] = states
        rowbuf[h, p] = jnp.dot(pick, states, preferred_element_type=jnp.float32).astype(jnp.bfloat16)
        for k in range(1, n_phase):
            row_copies.append(
                send(
                    rowbuf.at[h, p],
                    rowbuf.at[h, p],
                    row_send.at[h, k - 1],
                    row_recv.at[h, k - 1],
                    {"phase": lax.rem(p + k, n_phase)},
                )
            )

    halo_spread(1)
    relay(0, 1)
    for dist in range(2, reach + 1):
        halo_spread(dist)
        halo_pass(dist - 1)
    for t in range(2, n_seq):
        relay(0, t)
    if heads > 1:
        issue_own(1)
    halo_pass(reach)
    for k in range(1, n_phase):
        up_copies[k - 1].wait_recv()
        piece = upbuf.at[lax.rem(p + n_phase - k, n_phase), up_half]
        up_twins.append(send(piece, piece, upp_send.at[k - 1], upp_recv.at[k - 1], twin_core))

    for h in range(heads):
        more = list(range(1, n_seq)) if h + 1 < heads else []
        finish(h)
        query = own_block(h)
        for dist in range(1, reach + 1):
            if more:
                relay(h + 1, more.pop(0))
            if h == 0:
                halo_norm(dist)
            earlier_block(h, dist, query)
        for t in more:
            relay(h + 1, t)
        if h + 2 < heads:
            issue_own(h + 2)
        close(h)

    own_up.wait()
    for twin in up_twins:
        twin.wait_recv()

    def piece(s):
        got = jnp.dot(
            jnp.concatenate([rowbuf[h, s] for h in range(heads)], axis=1),
            upbuf[s],
            preferred_element_type=jnp.float32,
        )
        return got.astype(jnp.bfloat16).astype(jnp.float32)

    projected = piece(p)
    for copy in row_copies:
        copy.wait_recv()
    for k in range(1, n_phase):
        projected = projected + piece(lax.rem(p + k, n_phase))
    sq = jnp.sum(projected * projected, axis=1, keepdims=True)
    sqbuf[p] = jnp.broadcast_to(sq, (crows, crows)).T[0:8, :]
    sq_copies = []
    for k in range(1, n_phase):
        other = lax.rem(p + k, n_phase)
        sq_copies.append(
            send(sqbuf.at[p], sqbuf.at[p], sq_send.at[k - 1], sq_recv.at[k - 1], {"phase": other})
        )
    for copy in sq_copies:
        copy.wait_recv()
    all_sq = sqbuf[0]
    for k in range(1, n_phase):
        all_sq = all_sq + sqbuf[k]
    all_sq = jnp.broadcast_to(all_sq[0:1, :], (crows, crows)).T[:, 0:1]
    norm = lax.rsqrt(all_sq / (n_phase * cols) + 1e-05)
    main_in = (projected * norm * og_ref[...]).astype(jnp.bfloat16)
    routed = jnp.dot(place, main_in, preferred_element_type=jnp.float32).astype(jnp.bfloat16)
    for s in range(n_seq):
        outbuf[s] = routed[s * slot : (s + 1) * slot]
    a_copies = []
    for k in range(1, n_seq):
        other = lax.rem(z + k, n_seq)
        a_copies.append(
            send(outbuf.at[other], ss_ref.at[z], a_send.at[k - 1], a_recv.at[k - 1], {"seq": other})
        )
    ss_ref[z] = outbuf[z]
    for copy in a_copies:
        copy.wait_recv()
    for cond, copy in pending:
        when(cond, copy.wait_send)


def fused(n_seq, n_phase, byte_embed, in_gain, w_qkv, w_up, out_gain, bounds, owner):
    tok, d = byte_embed.shape
    rows, _, width = w_qkv.shape
    heads = width // HD
    crows = bounds.shape[0]
    cols = out_gain.shape[0]
    slot = 2 * crows // n_seq
    reach = -(-WINDOW // tok)
    bf, f32 = jnp.bfloat16, jnp.float32
    vmem = pl.BlockSpec(memory_space=pltpu.VMEM)
    hbm = pl.BlockSpec(memory_space=pltpu.HBM)
    dma = pltpu.SemaphoreType.DMA
    states, stretch = pl.pallas_call(
        functools.partial(fused_kernel, (n_seq, n_phase, reach, slot)),
        out_shape=(
            jax.ShapeDtypeStruct((tok, width), bf),
            jax.ShapeDtypeStruct((n_seq, slot, cols), bf),
        ),
        in_specs=[hbm, vmem, hbm, hbm, vmem, vmem, vmem],
        out_specs=(vmem, vmem),
        scratch_shapes=[
            pltpu.VMEM((tok, d), bf),
            pltpu.VMEM((tok, d), bf),
            pltpu.VMEM((reach, n_phase, tok, width), bf),
            pltpu.VMEM((reach, tok, d), bf),
            pltpu.VMEM((heads, 3, n_seq * rows, HD), bf),
            pltpu.VMEM((n_phase, w_up.shape[0], cols), bf),
            pltpu.VMEM((reach + 1, tok, HD), bf),
            pltpu.VMEM((reach + 1, tok, HD), bf),
            pltpu.VMEM((tok, HD), f32),
            pltpu.VMEM((tok, 1), f32),
            pltpu.VMEM((tok, 1), f32),
            pltpu.VMEM((heads, n_phase, crows, HD), bf),
            pltpu.VMEM((n_phase, 8, crows), f32),
            pltpu.VMEM((n_seq, slot, cols), bf),
            dma((2 + heads,)),
            dma((2, heads, n_seq - 1)),
            dma((2, heads, n_seq - 1)),
            dma((2, heads, n_seq - 1)),
            dma((2, heads, n_seq - 1)),
            dma((n_phase - 1,)),
            dma((n_phase - 1,)),
            dma((n_phase - 1,)),
            dma((n_phase - 1,)),
            dma((reach,)),
            dma((reach,)),
            dma((reach, 4)),
            dma((reach, 4)),
            dma((heads, n_phase - 1)),
            dma((heads, n_phase - 1)),
            dma((n_phase - 1,)),
            dma((n_phase - 1,)),
            dma((n_seq - 1,)),
            dma((n_seq - 1,)),
        ],
        compiler_params=pltpu.CompilerParams(
            collective_id=0, has_side_effects=True, vmem_limit_bytes=56 * 1024 * 1024
        ),
    )(
        byte_embed,
        in_gain.reshape(1, d),
        jnp.transpose(w_qkv, (1, 0, 2)),
        w_up,
        out_gain.reshape(1, cols),
        bounds.reshape(1, crows),
        owner.reshape(1, crows),
    )
    return states, stretch.reshape(n_seq * slot, cols)


def passed_along(value, axis, by):
    devices = lax.axis_size(axis)
    pairs = [(i, i + by) for i in range(devices) if 0 <= i + by < devices]
    return lax.ppermute(value, axis, pairs)


def project_rows(rows, w_up, out_gain):
    groups = lax.axis_size("phase")
    full_rows = lax.all_gather(rows, "phase", axis=1, tiled=True)
    w_cols = lax.all_to_all(w_up, "phase", split_axis=1, concat_axis=0, tiled=True)
    count = full_rows.shape[0]
    width = rows.shape[1]
    columns = w_cols.shape[1]
    pieces = jnp.einsum(
        "nsg,sgc->snc",
        full_rows.reshape(count, groups, width),
        w_cols.reshape(groups, width, columns),
        preferred_element_type=jnp.float32,
    )
    projected = jnp.sum(pieces.astype(jnp.bfloat16).astype(jnp.float32), axis=0)
    squares = lax.psum(jnp.sum(projected * projected, axis=1), "phase")
    scale = lax.rsqrt(squares / DC + 1e-05)
    return (projected * scale[:, None] * out_gain).astype(jnp.bfloat16)


def on_device(byte_embed, in_gain, w_qkv, w_up, out_gain, bounds, owner):
    tok = byte_embed.shape[0]
    n_seq = lax.axis_size("seq")
    mine = lax.axis_index("seq")
    section = lax.axis_index("phase")
    width_dev = w_qkv.shape[2]
    heads_dev = width_dev // HD
    x32 = byte_embed.astype(jnp.float32)
    normed = (x32 * lax.rsqrt(jnp.mean(x32 * x32, axis=1, keepdims=True) + 1e-05) * in_gain).astype(
        jnp.bfloat16
    )
    piece = lax.all_gather(w_qkv, "seq", axis=0, tiled=True)
    qkv = jnp.dot(
        normed, piece.reshape(piece.shape[0], 3 * width_dev), preferred_element_type=jnp.float32
    ).astype(jnp.bfloat16)
    qkv = qkv.reshape(tok, 3, heads_dev, HD)
    query = qkv[:, 0]
    keys = qkv[:, 1]
    values = qkv[:, 2]
    reach = -(-WINDOW // tok)
    key_list = [keys]
    value_list = [values]
    for distance in range(1, reach + 1):
        earlier_keys, earlier_values = passed_along((keys, values), "seq", distance)
        key_list = [earlier_keys] + key_list
        value_list = [earlier_values] + value_list
    key_all = jnp.concatenate(key_list, axis=0)
    value_all = jnp.concatenate(value_list, axis=0)
    scores = jnp.einsum(
        "ihd,jhd->hij", query, key_all, preferred_element_type=jnp.float32
    ) * HD ** (-0.5)
    q_pos = mine * tok + jnp.arange(tok, dtype=jnp.int32)
    k_pos = mine * tok - reach * tok + jnp.arange((reach + 1) * tok, dtype=jnp.int32)
    keep = (
        (k_pos[None, :] <= q_pos[:, None])
        & (k_pos[None, :] > q_pos[:, None] - WINDOW)
        & (k_pos[None, :] >= 0)
    )
    scores = jnp.where(keep[None], scores, -jnp.inf)
    top = jnp.max(scores, axis=2, keepdims=True)
    expo = jnp.exp(scores - top)
    probs = (expo / jnp.sum(expo, axis=2, keepdims=True)).astype(jnp.bfloat16)
    attended = jnp.einsum(
        "hij,jhd->ihd", probs, value_all, preferred_element_type=jnp.float32
    ).astype(jnp.bfloat16)
    attended = attended.reshape(tok, width_dev)
    residual = lax.dynamic_slice_in_dim(x32, section * width_dev, width_dev, 1)
    byte_states = (residual + attended.astype(jnp.float32)).astype(jnp.bfloat16)
    local = bounds - mine * tok
    stretch_rows = jnp.take(byte_states, local, axis=0)
    owners = owner[:, 0]
    crows = owners.shape[0]
    slot_count = 2 * crows // n_seq
    place = jnp.arange(crows, dtype=jnp.int32)
    earlier = (owners[:, None] == owners[None, :]) & (place[None, :] < place[:, None])
    rank = jnp.sum(earlier.astype(jnp.int32), axis=1)
    target = owners * slot_count + rank
    placing = (target[None, :] == jnp.arange(n_seq * slot_count, dtype=jnp.int32)[:, None]).astype(
        jnp.bfloat16
    )
    outgoing = jnp.dot(placing, stretch_rows, preferred_element_type=jnp.float32).astype(
        jnp.bfloat16
    )
    outgoing = outgoing.reshape(n_seq, slot_count, width_dev)
    arrived = lax.all_to_all(outgoing, "seq", split_axis=0, concat_axis=0, tiled=True).reshape(
        n_seq * slot_count, width_dev
    )
    stretch_states = project_rows(arrived, w_up, out_gain)
    return (byte_states, stretch_states)


def solution(mesh):
    n_seq, n_phase, n_dp = (mesh.shape[axis] for axis in ("seq", "phase", "dp"))

    def body(byte_embed, in_gain, w_qkv, *rest):
        tok, (rows, _, width) = byte_embed.shape[0], w_qkv.shape
        slot = 2 * rest[2].shape[0] // n_seq
        tiled = rows % 128 == 0 and width % HD == 0 and tok % 256 == 0 and slot % 16 == 0
        if tiled and n_dp == 2 and n_phase == 4 and w_qkv.shape[0] == rest[0].shape[0]:
            return fused(n_seq, n_phase, byte_embed, in_gain, w_qkv, *rest)
        return on_device(byte_embed, in_gain, w_qkv, *rest)

    return jax.shard_map(
        body,
        mesh=mesh,
        in_specs=(
            P(("dp", "seq"), None),
            P(),
            P("seq", None, "phase"),
            P("phase", None),
            P("phase"),
            P(("dp", "seq")),
            P(("dp", "seq"), None),
        ),
        out_specs=(P(("dp", "seq"), "phase"), P(("dp", "seq"), "phase")),
        check_vma=False,
    )
```

```python
import functools
import math
import jax
import jax.numpy as jnp
from jax import lax
from jax.experimental import pallas as pl
from jax.experimental.pallas import tpu as pltpu
from jax.sharding import PartitionSpec as P

DC = 3072
HD = 128
WINDOW = 1024
MESH = pl.DeviceIdType.MESH
NEG = -0.7 * 3.4e38


def fused_kernel(
    dims,
    x_ref,
    gain_ref,
    w_ref,
    up_ref,
    og_ref,
    bounds_ref,
    owner_ref,
    bs_ref,
    ss_ref,
    xbuf,
    normed,
    halo,
    nhalo,
    wbuf,
    upbuf,
    kbuf,
    vbuf,
    obuf,
    mbuf,
    lbuf,
    rowbuf,
    sqbuf,
    outbuf,
    loc_sem,
    w_send,
    w_recv,
    p_send,
    p_recv,
    up_send,
    up_recv,
    upp_send,
    upp_recv,
    h_send,
    h_recv,
    g_send,
    g_recv,
    row_send,
    row_recv,
    sq_send,
    sq_recv,
    a_send,
    a_recv,
):
    n_seq, n_phase, reach, slot = dims
    tok, d = xbuf.shape
    rows, width = w_ref.shape[1:]
    half = rows // 2
    heads = width // HD
    crows = bounds_ref.shape[1]
    cols = og_ref.shape[1]
    z = lax.axis_index("seq")
    p = lax.axis_index("phase")
    c = lax.axis_index("dp")

    own_x = pltpu.make_async_copy(x_ref, xbuf, loc_sem.at[0])
    own_x.start()
    own_up = pltpu.make_async_copy(
        up_ref.at[:, pl.ds(pl.multiple_of(p * cols, 128), cols)], upbuf.at[p], loc_sem.at[1]
    )
    own_up.start()
    own_w = []
    for h in range(heads):
        own_w.append(
            pltpu.make_async_copy(
                w_ref.at[:, :, pl.ds(h * HD, HD)],
                wbuf.at[h, :, pl.ds(pl.multiple_of(z * rows, rows), rows), :],
                loc_sem.at[2 + h],
            )
        )
        own_w[h].start()

    twin_core = {"dp": 1 - c}
    peers = (
        [{"seq": lax.rem(z + k, n_seq)} for k in range(1, n_seq)]
        + [{"phase": lax.rem(p + k, n_phase)} for k in range(1, n_phase)]
        + [twin_core]
    )
    barrier = pltpu.get_barrier_semaphore()
    for peer in peers:
        pl.semaphore_signal(barrier, inc=1, device_id=peer, device_id_type=MESH)
    pl.semaphore_wait(barrier, len(peers))

    pending = []

    def when(cond, action):
        if cond is None:
            action()
        else:
            pl.when(cond)(action)

    def send(src, dst, ssem, rsem, peer, cond=None):
        copy = pltpu.make_async_remote_copy(
            src_ref=src, dst_ref=dst, send_sem=ssem, recv_sem=rsem, device_id=peer, device_id_type=MESH
        )
        when(cond, copy.start)
        pending.append((cond, copy))
        return copy

    right, left = {"seq": z + 1}, {"seq": z - 1}
    has_right, has_left = z < n_seq - 1, z > 0
    ways = ((right, has_right, -1), (left, has_left, 1))

    def chunk(h, shard):
        at = pl.multiple_of(shard * rows + c * half, half)
        return wbuf.at[h, :, pl.ds(at, half), :]

    def issue_own(h):
        if h >= heads or h in issued:
            return
        issued.add(h)
        src = w_ref.at[:, pl.ds(pl.multiple_of(c * half, half), half), pl.ds(h * HD, HD)]
        for way, (peer, cond, sign) in enumerate(ways):
            send(src, chunk(h, z), w_send.at[way, h, 0], w_recv.at[way, h, 0], peer, cond)

    twins = {}
    issued = set()
    LEFTWARD, RIGHTWARD = 1, 0

    def relay(h, t, *which):
        for way in which:
            if h >= heads or t >= n_seq or (h, t, way) in twins:
                continue
            peer, cond, sign = ways[way]
            shard = z + sign * t
            there = (shard >= 0) & (shard < n_seq)
            piece = chunk(h, jnp.clip(shard, 0, n_seq - 1))
            got = pltpu.make_async_remote_copy(
                src_ref=piece,
                dst_ref=piece,
                send_sem=w_send.at[way, h, t - 1],
                recv_sem=w_recv.at[way, h, t - 1],
                device_id=peer,
                device_id_type=MESH,
            )
            pl.when(there)(got.wait_recv)
            if t < n_seq - 1:
                send(piece, piece, w_send.at[way, h, t], w_recv.at[way, h, t], peer, there & cond)
            twins[h, t, way] = (
                there,
                send(piece, piece, p_send.at[way, h, t - 1], p_recv.at[way, h, t - 1], twin_core, there),
            )

    def finish(h):
        own_w[h].wait()
        for t in range(1, n_seq):
            relay(h, t, LEFTWARD, RIGHTWARD)
        for t in range(1, n_seq):
            for way in range(2):
                there, twin = twins[h, t, way]
                pl.when(there)(twin.wait_recv)

    across = {1: {"phase": p + 1 - 2 * lax.rem(p, 2)}, 2: {"phase": lax.rem(p + 2, n_phase)}}
    spots = {k: v["phase"] for k, v in across.items()}
    mine = {}

    def halo_start(dist, cond):
        src = x_ref.at[:, pl.ds(pl.multiple_of(p * width, 128), width)] if dist == 1 else halo.at[dist - 2, p]
        mine[dist] = send(src, halo.at[dist - 1, p], h_send.at[dist - 1], h_recv.at[dist - 1], right, cond)

    gathers = {}

    def halo_spread(dist):
        there = z >= dist
        pl.when(there)(mine[dist].wait_recv)
        if dist < reach:
            halo_start(dist + 1, there & has_right)
        for k in (1, 2):
            piece = halo.at[dist - 1, p]
            gathers[dist, k] = send(
                piece, piece, g_send.at[dist - 1, k - 1], g_recv.at[dist - 1, k - 1], across[k], there
            )

    def halo_pass(dist):
        there = z >= dist
        for k in (1, 2):
            pl.when(there)(gathers[dist, k].wait_recv)
            part = pl.ds((k - 1) * (tok // 2), tok // 2)
            piece = halo.at[dist - 1, spots[k], part]
            gathers[dist, 2 + k] = send(
                piece, piece, g_send.at[dist - 1, k + 1], g_recv.at[dist - 1, k + 1], across[3 - k], there
            )

    step_rows = 64

    def halo_norm(dist):
        @pl.when(z >= dist)
        def _():
            for k in (1, 2):
                gathers[dist, 2 + k].wait_recv()

            @pl.loop(0, tok // step_rows)
            def _(i):
                r = pl.ds(pl.multiple_of(i * step_rows, step_rows), step_rows)
                xx = jnp.concatenate([halo[dist - 1, s, r, :] for s in range(n_phase)], axis=1).astype(
                    jnp.float32
                )
                scale = lax.rsqrt(jnp.mean(xx * xx, axis=1, keepdims=True) + 1e-05)
                nhalo[dist - 1, r, :] = (xx * scale * gain_ref[...]).astype(jnp.bfloat16)

    halo_start(1, has_right)
    issue_own(0)
    up_rows = up_ref.shape[0] // 2
    up_half = pl.ds(pl.multiple_of(c * up_rows, up_rows), up_rows)
    up_copies, up_twins = [], []
    for k in range(1, n_phase):
        other = lax.rem(p + k, n_phase)
        part = pl.ds(pl.multiple_of(other * cols, 128), cols)
        up_copies.append(
            send(
                up_ref.at[up_half, part],
                upbuf.at[p, up_half],
                up_send.at[k - 1],
                up_recv.at[k - 1],
                {"phase": other},
            )
        )

    own_x.wait()

    @pl.loop(0, tok // step_rows)
    def _(i):
        r = pl.ds(pl.multiple_of(i * step_rows, step_rows), step_rows)
        xx = xbuf[r, :].astype(jnp.float32)
        scale = lax.rsqrt(jnp.mean(xx * xx, axis=1, keepdims=True) + 1e-05)
        normed[r, :] = (xx * scale * gain_ref[...]).astype(jnp.bfloat16)

    def column(ref):
        wide = jnp.broadcast_to(ref[...].astype(jnp.float32), (crows, crows))
        return wide.T

    local = column(bounds_ref)[:, 0:1] - (z * tok).astype(jnp.float32)
    spot = lax.broadcasted_iota(jnp.int32, (crows, tok), 1).astype(jnp.float32)
    pick = jnp.where(local == spot, 1.0, 0.0).astype(jnp.bfloat16)
    same = column(owner_ref) == owner_ref[...].astype(jnp.float32)
    before = lax.broadcasted_iota(jnp.int32, (crows, crows), 0) < lax.broadcasted_iota(
        jnp.int32, (crows, crows), 1
    )
    rank = jnp.sum(jnp.where(same & before, 1, 0), axis=0, keepdims=True)
    target = owner_ref[...] * slot + rank
    place = jnp.where(
        target == lax.broadcasted_iota(jnp.int32, (n_seq * slot, crows), 0), 1.0, 0.0
    ).astype(jnp.bfloat16)

    tq = min(tok, 256)
    scale = HD ** (-0.5) * math.log2(math.e)

    def attend(dist, query):
        for q0 in range(0, tok, tq):
            r = pl.ds(q0, tq)
            keys = tok if dist else q0 + tq
            s = lax.dot_general(
                query[q0 : q0 + tq],
                kbuf[dist, :keys],
                (((1,), (1,)), ((), ())),
                preferred_element_type=jnp.float32,
            )
            if dist == 0 or (dist + 1) * tok - 1 >= WINDOW:
                qi = q0 + lax.broadcasted_iota(jnp.int32, s.shape, 0)
                kj = lax.broadcasted_iota(jnp.int32, s.shape, 1) - dist * tok
                s = jnp.where((kj <= qi) & (kj > qi - WINDOW), s, NEG)
            top = jnp.max(s, axis=1, keepdims=True)
            if dist > 0:
                old = mbuf[r, :]
                top = jnp.maximum(top, old)
            e = jnp.exp2(s * scale - top * scale)
            total = jnp.sum(e, axis=1, keepdims=True)
            o = jnp.dot(e.astype(jnp.bfloat16), vbuf[dist, :keys], preferred_element_type=jnp.float32)
            if dist > 0:
                fade = jnp.exp2((old - top) * scale)
                total = total + fade * lbuf[r, :]
                o = o + fade * obuf[r, :]
            mbuf[r, :] = top
            lbuf[r, :] = total
            obuf[r, :] = o

    def own_block(h):
        w = jnp.concatenate([wbuf[h, j] for j in range(3)], axis=1)
        got = jnp.dot(normed[...], w, preferred_element_type=jnp.float32).astype(jnp.bfloat16)
        qbuf = got[:, :HD]
        kbuf[0] = got[:, HD : 2 * HD]
        vbuf[0] = got[:, 2 * HD :]
        attend(0, qbuf)
        return qbuf

    def earlier_block(h, dist, query):
        @pl.when(z >= dist)
        def _():
            w = jnp.concatenate([wbuf[h, j] for j in range(1, 3)], axis=1)
            got = jnp.dot(nhalo[dist - 1], w, preferred_element_type=jnp.float32).astype(jnp.bfloat16)
            kbuf[dist] = got[:, :HD]
            vbuf[dist] = got[:, HD:]
            attend(dist, query)

    row_copies = []

    def close(h):
        at = slice(h * HD, (h + 1) * HD)
        res = xbuf[:, pl.ds(pl.multiple_of(p * width + h * HD, HD), HD)].astype(jnp.float32)
        att = (obuf[...] / lbuf[...]).astype(jnp.bfloat16).astype(jnp.float32)
        states = (res + att).astype(jnp.bfloat16)
        bs_ref[:, at] = states
        rowbuf[h, p] = jnp.dot(pick, states, preferred_element_type=jnp.float32).astype(jnp.bfloat16)
        for k in range(1, n_phase):
            row_copies.append(
                send(
                    rowbuf.at[h, p],
                    rowbuf.at[h, p],
                    row_send.at[h, k - 1],
                    row_recv.at[h, k - 1],
                    {"phase": lax.rem(p + k, n_phase)},
                )
            )

    relay(0, 1, LEFTWARD)
    halo_spread(1)
    issue_own(1)
    relay(0, 1, RIGHTWARD)
    for t in range(2, n_seq):
        relay(0, t, LEFTWARD)
    for dist in range(2, reach + 1):
        halo_spread(dist)
        halo_pass(dist - 1)
    relay(1, 1, LEFTWARD, RIGHTWARD)
    issue_own(2)
    relay(0, 2, RIGHTWARD)
    for k in range(1, n_phase):
        up_copies[k - 1].wait_recv()
        piece = upbuf.at[lax.rem(p + n_phase - k, n_phase), up_half]
        up_twins.append(send(piece, piece, upp_send.at[k - 1], upp_recv.at[k - 1], twin_core))
    for t in range(2, n_seq):
        relay(1, t, LEFTWARD)

    for h in range(heads):
        issue_own(h + 1)
        finish(h)
        query = own_block(h)
        relay(h + 2, 1, LEFTWARD, RIGHTWARD)
        if h == 0:
            halo_pass(reach)
        relay(h + 1, 2, LEFTWARD, RIGHTWARD)
        for dist in range(1, reach + 1):
            if h == 0:
                halo_norm(dist)
            earlier_block(h, dist, query)
        relay(h + 2, 2, LEFTWARD, RIGHTWARD)
        issue_own(h + 3)
        close(h)

    own_up.wait()
    for twin in up_twins:
        twin.wait_recv()

    def piece(s):
        got = jnp.dot(
            jnp.concatenate([rowbuf[h, s] for h in range(heads)], axis=1),
            upbuf[s],
            preferred_element_type=jnp.float32,
        )
        return got.astype(jnp.bfloat16).astype(jnp.float32)

    projected = piece(p)
    for copy in row_copies:
        copy.wait_recv()
    for k in range(1, n_phase):
        projected = projected + piece(lax.rem(p + k, n_phase))
    sq = jnp.sum(projected * projected, axis=1, keepdims=True)
    sqbuf[p] = jnp.broadcast_to(sq, (crows, crows)).T[0:8, :]
    sq_copies = []
    for k in range(1, n_phase):
        other = lax.rem(p + k, n_phase)
        sq_copies.append(
            send(sqbuf.at[p], sqbuf.at[p], sq_send.at[k - 1], sq_recv.at[k - 1], {"phase": other})
        )
    for copy in sq_copies:
        copy.wait_recv()
    all_sq = sqbuf[0]
    for k in range(1, n_phase):
        all_sq = all_sq + sqbuf[k]
    all_sq = jnp.broadcast_to(all_sq[0:1, :], (crows, crows)).T[:, 0:1]
    norm = lax.rsqrt(all_sq / (n_phase * cols) + 1e-05)
    main_in = (projected * norm * og_ref[...]).astype(jnp.bfloat16)
    routed = jnp.dot(place, main_in, preferred_element_type=jnp.float32).astype(jnp.bfloat16)
    for s in range(n_seq):
        outbuf[s] = routed[s * slot : (s + 1) * slot]
    a_copies = []
    for k in range(1, n_seq):
        other = lax.rem(z + k, n_seq)
        a_copies.append(
            send(outbuf.at[other], ss_ref.at[z], a_send.at[k - 1], a_recv.at[k - 1], {"seq": other})
        )
    ss_ref[z] = outbuf[z]
    for copy in a_copies:
        copy.wait_recv()
    for cond, copy in pending:
        when(cond, copy.wait_send)


def fused(n_seq, n_phase, byte_embed, in_gain, w_qkv, w_up, out_gain, bounds, owner):
    tok, d = byte_embed.shape
    rows, _, width = w_qkv.shape
    heads = width // HD
    crows = bounds.shape[0]
    cols = out_gain.shape[0]
    slot = 2 * crows // n_seq
    reach = -(-WINDOW // tok)
    bf, f32 = jnp.bfloat16, jnp.float32
    vmem = pl.BlockSpec(memory_space=pltpu.VMEM)
    hbm = pl.BlockSpec(memory_space=pltpu.HBM)
    dma = pltpu.SemaphoreType.DMA
    states, stretch = pl.pallas_call(
        functools.partial(fused_kernel, (n_seq, n_phase, reach, slot)),
        out_shape=(
            jax.ShapeDtypeStruct((tok, width), bf),
            jax.ShapeDtypeStruct((n_seq, slot, cols), bf),
        ),
        in_specs=[hbm, vmem, hbm, hbm, vmem, vmem, vmem],
        out_specs=(vmem, vmem),
        scratch_shapes=[
            pltpu.VMEM((tok, d), bf),
            pltpu.VMEM((tok, d), bf),
            pltpu.VMEM((reach, n_phase, tok, width), bf),
            pltpu.VMEM((reach, tok, d), bf),
            pltpu.VMEM((heads, 3, n_seq * rows, HD), bf),
            pltpu.VMEM((n_phase, w_up.shape[0], cols), bf),
            pltpu.VMEM((reach + 1, tok, HD), bf),
            pltpu.VMEM((reach + 1, tok, HD), bf),
            pltpu.VMEM((tok, HD), f32),
            pltpu.VMEM((tok, 1), f32),
            pltpu.VMEM((tok, 1), f32),
            pltpu.VMEM((heads, n_phase, crows, HD), bf),
            pltpu.VMEM((n_phase, 8, crows), f32),
            pltpu.VMEM((n_seq, slot, cols), bf),
            dma((2 + heads,)),
            dma((2, heads, n_seq - 1)),
            dma((2, heads, n_seq - 1)),
            dma((2, heads, n_seq - 1)),
            dma((2, heads, n_seq - 1)),
            dma((n_phase - 1,)),
            dma((n_phase - 1,)),
            dma((n_phase - 1,)),
            dma((n_phase - 1,)),
            dma((reach,)),
            dma((reach,)),
            dma((reach, 4)),
            dma((reach, 4)),
            dma((heads, n_phase - 1)),
            dma((heads, n_phase - 1)),
            dma((n_phase - 1,)),
            dma((n_phase - 1,)),
            dma((n_seq - 1,)),
            dma((n_seq - 1,)),
        ],
        compiler_params=pltpu.CompilerParams(
            collective_id=0, has_side_effects=True, vmem_limit_bytes=36 * 1024 * 1024
        ),
    )(
        pltpu.with_memory_space_constraint(byte_embed, pltpu.HBM),
        in_gain.reshape(1, d),
        pltpu.with_memory_space_constraint(jnp.transpose(w_qkv, (1, 0, 2)), pltpu.HBM),
        pltpu.with_memory_space_constraint(w_up, pltpu.HBM),
        out_gain.reshape(1, cols),
        bounds.reshape(1, crows),
        owner.reshape(1, crows),
    )
    return states, stretch.reshape(n_seq * slot, cols)


def passed_along(value, axis, by):
    devices = lax.axis_size(axis)
    pairs = [(i, i + by) for i in range(devices) if 0 <= i + by < devices]
    return lax.ppermute(value, axis, pairs)


def project_rows(rows, w_up, out_gain):
    groups = lax.axis_size("phase")
    full_rows = lax.all_gather(rows, "phase", axis=1, tiled=True)
    w_cols = lax.all_to_all(w_up, "phase", split_axis=1, concat_axis=0, tiled=True)
    count = full_rows.shape[0]
    width = rows.shape[1]
    columns = w_cols.shape[1]
    pieces = jnp.einsum(
        "nsg,sgc->snc",
        full_rows.reshape(count, groups, width),
        w_cols.reshape(groups, width, columns),
        preferred_element_type=jnp.float32,
    )
    projected = jnp.sum(pieces.astype(jnp.bfloat16).astype(jnp.float32), axis=0)
    squares = lax.psum(jnp.sum(projected * projected, axis=1), "phase")
    scale = lax.rsqrt(squares / DC + 1e-05)
    return (projected * scale[:, None] * out_gain).astype(jnp.bfloat16)


def on_device(byte_embed, in_gain, w_qkv, w_up, out_gain, bounds, owner):
    tok = byte_embed.shape[0]
    n_seq = lax.axis_size("seq")
    mine = lax.axis_index("seq")
    section = lax.axis_index("phase")
    width_dev = w_qkv.shape[2]
    heads_dev = width_dev // HD
    x32 = byte_embed.astype(jnp.float32)
    normed = (x32 * lax.rsqrt(jnp.mean(x32 * x32, axis=1, keepdims=True) + 1e-05) * in_gain).astype(
        jnp.bfloat16
    )
    piece = lax.all_gather(w_qkv, "seq", axis=0, tiled=True)
    qkv = jnp.dot(
        normed, piece.reshape(piece.shape[0], 3 * width_dev), preferred_element_type=jnp.float32
    ).astype(jnp.bfloat16)
    qkv = qkv.reshape(tok, 3, heads_dev, HD)
    query = qkv[:, 0]
    keys = qkv[:, 1]
    values = qkv[:, 2]
    reach = -(-WINDOW // tok)
    key_list = [keys]
    value_list = [values]
    for distance in range(1, reach + 1):
        earlier_keys, earlier_values = passed_along((keys, values), "seq", distance)
        key_list = [earlier_keys] + key_list
        value_list = [earlier_values] + value_list
    key_all = jnp.concatenate(key_list, axis=0)
    value_all = jnp.concatenate(value_list, axis=0)
    scores = jnp.einsum(
        "ihd,jhd->hij", query, key_all, preferred_element_type=jnp.float32
    ) * HD ** (-0.5)
    q_pos = mine * tok + jnp.arange(tok, dtype=jnp.int32)
    k_pos = mine * tok - reach * tok + jnp.arange((reach + 1) * tok, dtype=jnp.int32)
    keep = (
        (k_pos[None, :] <= q_pos[:, None])
        & (k_pos[None, :] > q_pos[:, None] - WINDOW)
        & (k_pos[None, :] >= 0)
    )
    scores = jnp.where(keep[None], scores, -jnp.inf)
    top = jnp.max(scores, axis=2, keepdims=True)
    expo = jnp.exp(scores - top)
    probs = (expo / jnp.sum(expo, axis=2, keepdims=True)).astype(jnp.bfloat16)
    attended = jnp.einsum(
        "hij,jhd->ihd", probs, value_all, preferred_element_type=jnp.float32
    ).astype(jnp.bfloat16)
    attended = attended.reshape(tok, width_dev)
    residual = lax.dynamic_slice_in_dim(x32, section * width_dev, width_dev, 1)
    byte_states = (residual + attended.astype(jnp.float32)).astype(jnp.bfloat16)
    local = bounds - mine * tok
    stretch_rows = jnp.take(byte_states, local, axis=0)
    owners = owner[:, 0]
    crows = owners.shape[0]
    slot_count = 2 * crows // n_seq
    place = jnp.arange(crows, dtype=jnp.int32)
    earlier = (owners[:, None] == owners[None, :]) & (place[None, :] < place[:, None])
    rank = jnp.sum(earlier.astype(jnp.int32), axis=1)
    target = owners * slot_count + rank
    placing = (target[None, :] == jnp.arange(n_seq * slot_count, dtype=jnp.int32)[:, None]).astype(
        jnp.bfloat16
    )
    outgoing = jnp.dot(placing, stretch_rows, preferred_element_type=jnp.float32).astype(
        jnp.bfloat16
    )
    outgoing = outgoing.reshape(n_seq, slot_count, width_dev)
    arrived = lax.all_to_all(outgoing, "seq", split_axis=0, concat_axis=0, tiled=True).reshape(
        n_seq * slot_count, width_dev
    )
    stretch_states = project_rows(arrived, w_up, out_gain)
    return (byte_states, stretch_states)


def solution(mesh):
    n_seq, n_phase, n_dp = (mesh.shape[axis] for axis in ("seq", "phase", "dp"))

    def body(byte_embed, in_gain, w_qkv, *rest):
        tok, (rows, _, width) = byte_embed.shape[0], w_qkv.shape
        slot = 2 * rest[2].shape[0] // n_seq
        tiled = rows % 128 == 0 and width % HD == 0 and tok % 256 == 0 and slot % 16 == 0
        if tiled and n_dp == 2 and n_phase == 4 and w_qkv.shape[0] == rest[0].shape[0]:
            return fused(n_seq, n_phase, byte_embed, in_gain, w_qkv, *rest)
        return on_device(byte_embed, in_gain, w_qkv, *rest)

    return jax.shard_map(
        body,
        mesh=mesh,
        in_specs=(
            P(("dp", "seq"), None),
            P(),
            P("seq", None, "phase"),
            P("phase", None),
            P("phase"),
            P(("dp", "seq")),
            P(("dp", "seq"), None),
        ),
        out_specs=(P(("dp", "seq"), "phase"), P(("dp", "seq"), "phase")),
        check_vma=False,
    )
```

```python
import functools
import math
import jax
import jax.numpy as jnp
from jax import lax
from jax.experimental import pallas as pl
from jax.experimental.pallas import tpu as pltpu
from jax.sharding import PartitionSpec as P

DC = 3072
HD = 128
WINDOW = 1024
MESH = pl.DeviceIdType.MESH
NEG = -0.7 * 3.4e38


def fused_kernel(
    dims,
    x_ref,
    gain_ref,
    w_ref,
    up_ref,
    og_ref,
    bounds_ref,
    owner_ref,
    bs_ref,
    ss_ref,
    xbuf,
    normed,
    halo,
    wbuf,
    upbuf,
    qbuf,
    kbuf,
    vbuf,
    obuf,
    mbuf,
    lbuf,
    rowbuf,
    sqbuf,
    outbuf,
    loc_sem,
    w_send,
    w_recv,
    p_send,
    p_recv,
    up_send,
    up_recv,
    upp_send,
    upp_recv,
    h_send,
    h_recv,
    g_send,
    g_recv,
    row_send,
    row_recv,
    sq_send,
    sq_recv,
    a_send,
    a_recv,
):
    n_seq, n_phase, reach, slot = dims
    tok, d = xbuf.shape
    rows, width = w_ref.shape[1:]
    half = rows // 2
    heads = width // HD
    crows = bounds_ref.shape[1]
    cols = og_ref.shape[1]
    z = lax.axis_index("seq")
    p = lax.axis_index("phase")
    c = lax.axis_index("dp")

    own_x = pltpu.make_async_copy(x_ref, xbuf, loc_sem.at[0])
    own_x.start()
    own_up = pltpu.make_async_copy(
        up_ref.at[:, pl.ds(pl.multiple_of(p * cols, 128), cols)], upbuf.at[p], loc_sem.at[1]
    )
    own_up.start()
    own_w = []
    for h in range(heads):
        own_w.append(
            pltpu.make_async_copy(
                w_ref.at[:, :, pl.ds(h * HD, HD)],
                wbuf.at[h, :, pl.ds(pl.multiple_of(z * rows, rows), rows), :],
                loc_sem.at[2 + h],
            )
        )
        own_w[h].start()

    twin_core = {"dp": 1 - c}
    peers = (
        [{"seq": lax.rem(z + k, n_seq)} for k in range(1, n_seq)]
        + [{"phase": lax.rem(p + k, n_phase)} for k in range(1, n_phase)]
        + [twin_core]
    )
    barrier = pltpu.get_barrier_semaphore()
    for peer in peers:
        pl.semaphore_signal(barrier, inc=1, device_id=peer, device_id_type=MESH)
    pl.semaphore_wait(barrier, len(peers))

    pending = []

    def when(cond, action):
        if cond is None:
            action()
        else:
            pl.when(cond)(action)

    def send(src, dst, ssem, rsem, peer, cond=None):
        copy = pltpu.make_async_remote_copy(
            src_ref=src, dst_ref=dst, send_sem=ssem, recv_sem=rsem, device_id=peer, device_id_type=MESH
        )
        when(cond, copy.start)
        pending.append((cond, copy))
        return copy

    right, left = {"seq": z + 1}, {"seq": z - 1}
    has_right, has_left = z < n_seq - 1, z > 0
    ways = ((right, has_right, -1), (left, has_left, 1))

    def chunk(h, shard):
        at = pl.multiple_of(shard * rows + c * half, half)
        return wbuf.at[h, :, pl.ds(at, half), :]

    def issue_own(h):
        if h >= heads or h in issued:
            return
        issued.add(h)
        src = w_ref.at[:, pl.ds(pl.multiple_of(c * half, half), half), pl.ds(h * HD, HD)]
        for way, (peer, cond, sign) in enumerate(ways):
            send(src, chunk(h, z), w_send.at[way, h, 0], w_recv.at[way, h, 0], peer, cond)

    twins = {}
    issued = set()
    LEFTWARD, RIGHTWARD = 1, 0

    def relay(h, t, *which):
        for way in which:
            if h >= heads or t >= n_seq or (h, t, way) in twins:
                continue
            peer, cond, sign = ways[way]
            shard = z + sign * t
            there = (shard >= 0) & (shard < n_seq)
            piece = chunk(h, jnp.clip(shard, 0, n_seq - 1))
            got = pltpu.make_async_remote_copy(
                src_ref=piece,
                dst_ref=piece,
                send_sem=w_send.at[way, h, t - 1],
                recv_sem=w_recv.at[way, h, t - 1],
                device_id=peer,
                device_id_type=MESH,
            )
            pl.when(there)(got.wait_recv)
            if t < n_seq - 1:
                send(piece, piece, w_send.at[way, h, t], w_recv.at[way, h, t], peer, there & cond)
            twins[h, t, way] = (
                there,
                send(piece, piece, p_send.at[way, h, t - 1], p_recv.at[way, h, t - 1], twin_core, there),
            )

    def finish(h):
        own_w[h].wait()
        for t in range(1, n_seq):
            relay(h, t, LEFTWARD, RIGHTWARD)
        for t in range(1, n_seq):
            for way in range(2):
                there, twin = twins[h, t, way]
                pl.when(there)(twin.wait_recv)

    across = {1: {"phase": p + 1 - 2 * lax.rem(p, 2)}, 2: {"phase": lax.rem(p + 2, n_phase)}}
    spots = {k: v["phase"] for k, v in across.items()}
    mine = {}

    def halo_start(dist, cond):
        own = normed.at[:, pl.ds(pl.multiple_of(p * width, 128), width)]
        src = own if dist == 1 else halo.at[dist - 2, p]
        mine[dist] = send(src, halo.at[dist - 1, p], h_send.at[dist - 1], h_recv.at[dist - 1], right, cond)

    gathers = {}

    def halo_spread(dist):
        there = z >= dist
        pl.when(there)(mine[dist].wait_recv)
        if dist < reach:
            halo_start(dist + 1, there & has_right)
        for k in (1, 2):
            piece = halo.at[dist - 1, p]
            gathers[dist, k] = send(
                piece, piece, g_send.at[dist - 1, k - 1], g_recv.at[dist - 1, k - 1], across[k], there
            )

    def halo_pass(dist):
        there = z >= dist
        for k in (1, 2):
            pl.when(there)(gathers[dist, k].wait_recv)
            part = pl.ds((k - 1) * (tok // 2), tok // 2)
            piece = halo.at[dist - 1, spots[k], part]
            gathers[dist, 2 + k] = send(
                piece, piece, g_send.at[dist - 1, k + 1], g_recv.at[dist - 1, k + 1], across[3 - k], there
            )

    def halo_wait(dist):
        @pl.when(z >= dist)
        def _():
            for k in (1, 2):
                gathers[dist, 2 + k].wait_recv()

    issue_own(0)
    up_rows = up_ref.shape[0] // 2
    up_half = pl.ds(pl.multiple_of(c * up_rows, up_rows), up_rows)
    up_copies, up_twins = [], []
    for k in range(1, n_phase):
        other = lax.rem(p + k, n_phase)
        part = pl.ds(pl.multiple_of(other * cols, 128), cols)
        up_copies.append(
            send(
                up_ref.at[up_half, part],
                upbuf.at[p, up_half],
                up_send.at[k - 1],
                up_recv.at[k - 1],
                {"phase": other},
            )
        )

    own_x.wait()
    step_rows = 64

    @pl.loop(0, tok // step_rows)
    def _(i):
        r = pl.ds(pl.multiple_of(i * step_rows, step_rows), step_rows)
        xx = xbuf[r, :].astype(jnp.float32)
        scale = lax.rsqrt(jnp.mean(xx * xx, axis=1, keepdims=True) + 1e-05)
        normed[r, :] = (xx * scale * gain_ref[...]).astype(jnp.bfloat16)

    relay(0, 1, LEFTWARD)
    halo_start(1, has_right)

    def column(ref):
        wide = jnp.broadcast_to(ref[...].astype(jnp.float32), (crows, crows))
        return wide.T

    local = column(bounds_ref)[:, 0:1] - (z * tok).astype(jnp.float32)
    spot = lax.broadcasted_iota(jnp.int32, (crows, tok), 1).astype(jnp.float32)
    pick = jnp.where(local == spot, 1.0, 0.0).astype(jnp.bfloat16)
    same = column(owner_ref) == owner_ref[...].astype(jnp.float32)
    before = lax.broadcasted_iota(jnp.int32, (crows, crows), 0) < lax.broadcasted_iota(
        jnp.int32, (crows, crows), 1
    )
    rank = jnp.sum(jnp.where(same & before, 1, 0), axis=0, keepdims=True)
    target = owner_ref[...] * slot + rank
    place = jnp.where(
        target == lax.broadcasted_iota(jnp.int32, (n_seq * slot, crows), 0), 1.0, 0.0
    ).astype(jnp.bfloat16)

    tq = min(tok, 256)
    scale = HD ** (-0.5) * math.log2(math.e)

    def attend(dist, h):
        for q0 in range(0, tok, tq):
            r = pl.ds(q0, tq)
            keys = tok if dist else q0 + tq
            s = lax.dot_general(
                qbuf[h, r, :],
                kbuf[dist, :keys],
                (((1,), (1,)), ((), ())),
                preferred_element_type=jnp.float32,
            )
            if dist == 0 or (dist + 1) * tok - 1 >= WINDOW:
                qi = q0 + lax.broadcasted_iota(jnp.int32, s.shape, 0)
                kj = lax.broadcasted_iota(jnp.int32, s.shape, 1) - dist * tok
                s = jnp.where((kj <= qi) & (kj > qi - WINDOW), s, NEG)
            top = jnp.max(s, axis=1, keepdims=True)
            if dist > 0:
                old = mbuf[h, r, :]
                top = jnp.maximum(top, old)
            e = jnp.exp2(s * scale - top * scale)
            total = jnp.sum(e, axis=1, keepdims=True)
            o = jnp.dot(e.astype(jnp.bfloat16), vbuf[dist, :keys], preferred_element_type=jnp.float32)
            if dist > 0:
                fade = jnp.exp2((old - top) * scale)
                total = total + fade * lbuf[h, r, :]
                o = o + fade * obuf[h, r, :]
            mbuf[h, r, :] = top
            lbuf[h, r, :] = total
            obuf[h, r, :] = o

    def own_block(h):
        w = jnp.concatenate([wbuf[h, j] for j in range(3)], axis=1)
        got = jnp.dot(normed[...], w, preferred_element_type=jnp.float32).astype(jnp.bfloat16)
        qbuf[h] = got[:, :HD]
        kbuf[0] = got[:, HD : 2 * HD]
        vbuf[0] = got[:, 2 * HD :]
        attend(0, h)

    def earlier_block(h, dist):
        @pl.when(z >= dist)
        def _():
            w = jnp.concatenate([wbuf[h, j] for j in range(1, 3)], axis=1)
            rows_in = jnp.concatenate([halo[dist - 1, q] for q in range(n_phase)], axis=1)
            got = jnp.dot(rows_in, w, preferred_element_type=jnp.float32).astype(jnp.bfloat16)
            kbuf[dist] = got[:, :HD]
            vbuf[dist] = got[:, HD:]
            attend(dist, h)

    row_copies = []

    def close(h):
        at = slice(h * HD, (h + 1) * HD)
        res = xbuf[:, pl.ds(pl.multiple_of(p * width + h * HD, HD), HD)].astype(jnp.float32)
        att = (obuf[h] / lbuf[h]).astype(jnp.bfloat16).astype(jnp.float32)
        states = (res + att).astype(jnp.bfloat16)
        bs_ref[:, at] = states
        rowbuf[h, p] = jnp.dot(pick, states, preferred_element_type=jnp.float32).astype(jnp.bfloat16)
        for k in range(1, n_phase):
            row_copies.append(
                send(
                    rowbuf.at[h, p],
                    rowbuf.at[h, p],
                    row_send.at[h, k - 1],
                    row_recv.at[h, k - 1],
                    {"phase": lax.rem(p + k, n_phase)},
                )
            )

    halo_spread(1)
    issue_own(1)
    relay(0, 1, RIGHTWARD)
    for t in range(2, n_seq):
        relay(0, t, LEFTWARD)
    for dist in range(2, reach + 1):
        halo_spread(dist)
        halo_pass(dist - 1)
    relay(1, 1, LEFTWARD, RIGHTWARD)
    issue_own(2)
    relay(0, 2, RIGHTWARD)
    for k in range(1, n_phase):
        up_copies[k - 1].wait_recv()
        piece = upbuf.at[lax.rem(p + n_phase - k, n_phase), up_half]
        up_twins.append(send(piece, piece, upp_send.at[k - 1], upp_recv.at[k - 1], twin_core))
    for t in range(2, n_seq):
        relay(1, t, LEFTWARD)

    for h in range(heads):
        issue_own(h + 1)
        finish(h)
        own_block(h)
        relay(h + 2, 1, LEFTWARD, RIGHTWARD)
        if h == 0:
            halo_pass(reach)
        relay(h + 1, 2, LEFTWARD, RIGHTWARD)
        for dist in range(1, reach):
            if h == 0:
                halo_wait(dist)
            earlier_block(h, dist)
        relay(h + 2, 2, LEFTWARD, RIGHTWARD)
        issue_own(h + 3)
    halo_wait(reach)
    for h in range(heads):
        earlier_block(h, reach)
        close(h)

    own_up.wait()
    for twin in up_twins:
        twin.wait_recv()

    def piece(s):
        got = jnp.dot(
            jnp.concatenate([rowbuf[h, s] for h in range(heads)], axis=1),
            upbuf[s],
            preferred_element_type=jnp.float32,
        )
        return got.astype(jnp.bfloat16).astype(jnp.float32)

    projected = piece(p)
    for copy in row_copies:
        copy.wait_recv()
    for k in range(1, n_phase):
        projected = projected + piece(lax.rem(p + k, n_phase))
    sq = jnp.sum(projected * projected, axis=1, keepdims=True)
    sqbuf[p] = jnp.broadcast_to(sq, (crows, crows)).T[0:8, :]
    sq_copies = []
    for k in range(1, n_phase):
        other = lax.rem(p + k, n_phase)
        sq_copies.append(
            send(sqbuf.at[p], sqbuf.at[p], sq_send.at[k - 1], sq_recv.at[k - 1], {"phase": other})
        )
    for copy in sq_copies:
        copy.wait_recv()
    all_sq = sqbuf[0]
    for k in range(1, n_phase):
        all_sq = all_sq + sqbuf[k]
    all_sq = jnp.broadcast_to(all_sq[0:1, :], (crows, crows)).T[:, 0:1]
    norm = lax.rsqrt(all_sq / (n_phase * cols) + 1e-05)
    main_in = (projected * norm * og_ref[...]).astype(jnp.bfloat16)
    routed = jnp.dot(place, main_in, preferred_element_type=jnp.float32).astype(jnp.bfloat16)
    for s in range(n_seq):
        outbuf[s] = routed[s * slot : (s + 1) * slot]
    a_copies = []
    for k in range(1, n_seq):
        other = lax.rem(z + k, n_seq)
        a_copies.append(
            send(outbuf.at[other], ss_ref.at[z], a_send.at[k - 1], a_recv.at[k - 1], {"seq": other})
        )
    ss_ref[z] = outbuf[z]
    for copy in a_copies:
        copy.wait_recv()
    for cond, copy in pending:
        when(cond, copy.wait_send)


def fused(n_seq, n_phase, byte_embed, in_gain, w_qkv, w_up, out_gain, bounds, owner):
    tok, d = byte_embed.shape
    rows, _, width = w_qkv.shape
    heads = width // HD
    crows = bounds.shape[0]
    cols = out_gain.shape[0]
    slot = 2 * crows // n_seq
    reach = -(-WINDOW // tok)
    bf, f32 = jnp.bfloat16, jnp.float32
    vmem = pl.BlockSpec(memory_space=pltpu.VMEM)
    hbm = pl.BlockSpec(memory_space=pltpu.HBM)
    dma = pltpu.SemaphoreType.DMA
    states, stretch = pl.pallas_call(
        functools.partial(fused_kernel, (n_seq, n_phase, reach, slot)),
        out_shape=(
            jax.ShapeDtypeStruct((tok, width), bf),
            jax.ShapeDtypeStruct((n_seq, slot, cols), bf),
        ),
        in_specs=[hbm, vmem, hbm, hbm, vmem, vmem, vmem],
        out_specs=(vmem, vmem),
        scratch_shapes=[
            pltpu.VMEM((tok, d), bf),
            pltpu.VMEM((tok, d), bf),
            pltpu.VMEM((reach, n_phase, tok, width), bf),
            pltpu.VMEM((heads, 3, n_seq * rows, HD), bf),
            pltpu.VMEM((n_phase, w_up.shape[0], cols), bf),
            pltpu.VMEM((heads, tok, HD), bf),
            pltpu.VMEM((reach + 1, tok, HD), bf),
            pltpu.VMEM((reach + 1, tok, HD), bf),
            pltpu.VMEM((heads, tok, HD), f32),
            pltpu.VMEM((heads, tok, 1), f32),
            pltpu.VMEM((heads, tok, 1), f32),
            pltpu.VMEM((heads, n_phase, crows, HD), bf),
            pltpu.VMEM((n_phase, 8, crows), f32),
            pltpu.VMEM((n_seq, slot, cols), bf),
            dma((2 + heads,)),
            dma((2, heads, n_seq - 1)),
            dma((2, heads, n_seq - 1)),
            dma((2, heads, n_seq - 1)),
            dma((2, heads, n_seq - 1)),
            dma((n_phase - 1,)),
            dma((n_phase - 1,)),
            dma((n_phase - 1,)),
            dma((n_phase - 1,)),
            dma((reach,)),
            dma((reach,)),
            dma((reach, 4)),
            dma((reach, 4)),
            dma((heads, n_phase - 1)),
            dma((heads, n_phase - 1)),
            dma((n_phase - 1,)),
            dma((n_phase - 1,)),
            dma((n_seq - 1,)),
            dma((n_seq - 1,)),
        ],
        compiler_params=pltpu.CompilerParams(
            collective_id=0, has_side_effects=True, vmem_limit_bytes=36 * 1024 * 1024
        ),
    )(
        pltpu.with_memory_space_constraint(byte_embed, pltpu.HBM),
        in_gain.reshape(1, d),
        pltpu.with_memory_space_constraint(jnp.transpose(w_qkv, (1, 0, 2)), pltpu.HBM),
        pltpu.with_memory_space_constraint(w_up, pltpu.HBM),
        out_gain.reshape(1, cols),
        bounds.reshape(1, crows),
        owner.reshape(1, crows),
    )
    return states, stretch.reshape(n_seq * slot, cols)


def passed_along(value, axis, by):
    devices = lax.axis_size(axis)
    pairs = [(i, i + by) for i in range(devices) if 0 <= i + by < devices]
    return lax.ppermute(value, axis, pairs)


def project_rows(rows, w_up, out_gain):
    groups = lax.axis_size("phase")
    full_rows = lax.all_gather(rows, "phase", axis=1, tiled=True)
    w_cols = lax.all_to_all(w_up, "phase", split_axis=1, concat_axis=0, tiled=True)
    count = full_rows.shape[0]
    width = rows.shape[1]
    columns = w_cols.shape[1]
    pieces = jnp.einsum(
        "nsg,sgc->snc",
        full_rows.reshape(count, groups, width),
        w_cols.reshape(groups, width, columns),
        preferred_element_type=jnp.float32,
    )
    projected = jnp.sum(pieces.astype(jnp.bfloat16).astype(jnp.float32), axis=0)
    squares = lax.psum(jnp.sum(projected * projected, axis=1), "phase")
    scale = lax.rsqrt(squares / DC + 1e-05)
    return (projected * scale[:, None] * out_gain).astype(jnp.bfloat16)


def on_device(byte_embed, in_gain, w_qkv, w_up, out_gain, bounds, owner):
    tok = byte_embed.shape[0]
    n_seq = lax.axis_size("seq")
    mine = lax.axis_index("seq")
    section = lax.axis_index("phase")
    width_dev = w_qkv.shape[2]
    heads_dev = width_dev // HD
    x32 = byte_embed.astype(jnp.float32)
    normed = (x32 * lax.rsqrt(jnp.mean(x32 * x32, axis=1, keepdims=True) + 1e-05) * in_gain).astype(
        jnp.bfloat16
    )
    piece = lax.all_gather(w_qkv, "seq", axis=0, tiled=True)
    qkv = jnp.dot(
        normed, piece.reshape(piece.shape[0], 3 * width_dev), preferred_element_type=jnp.float32
    ).astype(jnp.bfloat16)
    qkv = qkv.reshape(tok, 3, heads_dev, HD)
    query = qkv[:, 0]
    keys = qkv[:, 1]
    values = qkv[:, 2]
    reach = -(-WINDOW // tok)
    key_list = [keys]
    value_list = [values]
    for distance in range(1, reach + 1):
        earlier_keys, earlier_values = passed_along((keys, values), "seq", distance)
        key_list = [earlier_keys] + key_list
        value_list = [earlier_values] + value_list
    key_all = jnp.concatenate(key_list, axis=0)
    value_all = jnp.concatenate(value_list, axis=0)
    scores = jnp.einsum(
        "ihd,jhd->hij", query, key_all, preferred_element_type=jnp.float32
    ) * HD ** (-0.5)
    q_pos = mine * tok + jnp.arange(tok, dtype=jnp.int32)
    k_pos = mine * tok - reach * tok + jnp.arange((reach + 1) * tok, dtype=jnp.int32)
    keep = (
        (k_pos[None, :] <= q_pos[:, None])
        & (k_pos[None, :] > q_pos[:, None] - WINDOW)
        & (k_pos[None, :] >= 0)
    )
    scores = jnp.where(keep[None], scores, -jnp.inf)
    top = jnp.max(scores, axis=2, keepdims=True)
    expo = jnp.exp(scores - top)
    probs = (expo / jnp.sum(expo, axis=2, keepdims=True)).astype(jnp.bfloat16)
    attended = jnp.einsum(
        "hij,jhd->ihd", probs, value_all, preferred_element_type=jnp.float32
    ).astype(jnp.bfloat16)
    attended = attended.reshape(tok, width_dev)
    residual = lax.dynamic_slice_in_dim(x32, section * width_dev, width_dev, 1)
    byte_states = (residual + attended.astype(jnp.float32)).astype(jnp.bfloat16)
    local = bounds - mine * tok
    stretch_rows = jnp.take(byte_states, local, axis=0)
    owners = owner[:, 0]
    crows = owners.shape[0]
    slot_count = 2 * crows // n_seq
    place = jnp.arange(crows, dtype=jnp.int32)
    earlier = (owners[:, None] == owners[None, :]) & (place[None, :] < place[:, None])
    rank = jnp.sum(earlier.astype(jnp.int32), axis=1)
    target = owners * slot_count + rank
    placing = (target[None, :] == jnp.arange(n_seq * slot_count, dtype=jnp.int32)[:, None]).astype(
        jnp.bfloat16
    )
    outgoing = jnp.dot(placing, stretch_rows, preferred_element_type=jnp.float32).astype(
        jnp.bfloat16
    )
    outgoing = outgoing.reshape(n_seq, slot_count, width_dev)
    arrived = lax.all_to_all(outgoing, "seq", split_axis=0, concat_axis=0, tiled=True).reshape(
        n_seq * slot_count, width_dev
    )
    stretch_states = project_rows(arrived, w_up, out_gain)
    return (byte_states, stretch_states)


def solution(mesh):
    n_seq, n_phase, n_dp = (mesh.shape[axis] for axis in ("seq", "phase", "dp"))

    def body(byte_embed, in_gain, w_qkv, *rest):
        tok, (rows, _, width) = byte_embed.shape[0], w_qkv.shape
        slot = 2 * rest[2].shape[0] // n_seq
        tiled = rows % 128 == 0 and width % HD == 0 and tok % 256 == 0 and slot % 16 == 0
        if tiled and n_dp == 2 and n_phase == 4 and w_qkv.shape[0] == rest[0].shape[0]:
            return fused(n_seq, n_phase, byte_embed, in_gain, w_qkv, *rest)
        return on_device(byte_embed, in_gain, w_qkv, *rest)

    return jax.shard_map(
        body,
        mesh=mesh,
        in_specs=(
            P(("dp", "seq"), None),
            P(),
            P("seq", None, "phase"),
            P("phase", None),
            P("phase"),
            P(("dp", "seq")),
            P(("dp", "seq"), None),
        ),
        out_specs=(P(("dp", "seq"), "phase"), P(("dp", "seq"), "phase")),
        check_vma=False,
    )
```
